32 devices in a mesh: groups: 2 (over y), frames: 4 (over z), rows: 4 (over x, core).
Axes of the slice: x: 2, y: 2, z: 4, core: 2. Of those that a mesh axis runs over, the one named last changes fastest.
Arguments:
- latents: bfloat16 [16, 8, 16, 1280], P('rows', ('groups', 'frames')), parts along dimension 1, may hold values from -6 to 6
- spatial_weight: bfloat16 [3, 3, 1280, 1280], P(None, None, None, 'rows'), may hold values from -0.0546875 to 0.0546875
- spatial_bias: float32 [1280], P('rows'), may hold values from -3 to 3
- norm_gain: float32 [1280], P('rows'), may hold values from 0.1 to 1.9
- norm_shift: float32 [1280], P('rows'), may hold values from -3 to 3
- temporal_weight: bfloat16 [3, 1280, 1280], P(None, 'rows'), may hold values from -0.09375 to 0.09375
- temporal_bias: float32 [1280], replicated, may hold values from -3 to 3
- token_gain: float32 [1280], replicated, may hold values from 0.1 to 1.9
- query_weight: bfloat16 [1280, 1024], P(None, 'rows'), may hold values from -4 to 4
- key_weight: bfloat16 [1280, 1024], P(None, 'rows'), may hold values from -4 to 4
- value_weight: bfloat16 [1280, 1024], P(None, 'rows'), may hold values from -0.15625 to 0.15625
- output_weight: bfloat16 [1024, 1280], P('rows'), may hold values from -0.1875 to 0.1875
Outputs:
- denoised: bfloat16 [16, 8, 16, 1280], P('rows', ('groups', 'frames')), parts along dimension 1
The draws below stay inside these ranges and needn't reach their ends.
There are 2 independent parts, one for each index of `groups`. The reference program is written for one: setup_inputs(seed, part) draws one part's arguments, and reference() takes and returns one part's arrays. A program takes and returns all parts, laid end to end along the dimension named above; an argument that names none is the same for every part. Nothing has to cross between parts.
All inputs are finite; a program needn't handle non-finite values.
Results may differ from the reference program's by a relative error of at most 0.034.
Values may be sent and summed in bfloat16 or wider, within the bound.
A program may use at most 128 MiB of HBM per device.

```python
import math
import jax
import jax.numpy as jnp
from jax import lax

C = 1280
HEADS = 16
HD = 64
NORM_GROUPS = 32
LAT_H = 16
LAT_W = 16
FRAMES = 4
TOKENS = 1024


def shared_basis(key):
    base = jax.random.normal(jax.random.fold_in(key, 101), (C, HEADS * HD), jnp.float32)
    return jnp.clip(base, -5.0, 5.0) / math.sqrt(C)


def own_part(key, salt):
    noise = jax.random.normal(jax.random.fold_in(key, salt), (C, HEADS * HD), jnp.float32)
    return jnp.clip(noise, -5.0, 5.0) / math.sqrt(C)


def draw_query_weight(key, part):
    mixed = 0.6 * shared_basis(key) + 0.8 * own_part(key, 102)
    return jnp.clip(mixed, -4.0, 4.0).astype(jnp.bfloat16)


def draw_key_weight(key, part):
    mixed = 0.6 * shared_basis(key) + 0.8 * own_part(key, 103)
    return jnp.clip(mixed, -4.0, 4.0).astype(jnp.bfloat16)


def shard_levels(rng, dims, pieces, smallest, high):
    loudness, own = 1.0, jax.random.fold_in(rng, 6)
    for dim, shards_of in pieces:
        steps = jnp.exp(jax.random.uniform(jax.random.fold_in(own, dim), (shards_of,), jnp.float32, smallest / len(pieces), high / len(pieces)))
        loudness = loudness * jnp.repeat(steps, dims[dim] // shards_of).reshape([-1 if axis == dim else 1 for axis in range(len(dims))])
    return loudness


def normal_values(rng, shape, width, most, shards=(), kind=jnp.bfloat16):
    entries = width * jax.random.normal(rng, shape, jnp.float32)
    if shards:
        entries = entries * shard_levels(rng, shape, shards, -0.22, 0.18)
    return jnp.clip(entries, -most, most).astype(kind)


def setup_inputs(seed: int = 0, part: int = 0) -> dict:
    splits = jax.random.split(jax.random.key(seed), 13)
    part_splits = jax.random.split(jax.random.fold_in(splits[12], part), 13)
    return {
        "latents": normal_values(part_splits[0], (LAT_H, FRAMES, LAT_W, C), 1.0, 6.0, ((0, 4), (1, 4))),
        "spatial_weight": normal_values(splits[1], (3, 3, C, C), (9 * C) ** -0.5, 0.0546875, ((3, 4),)),
        "spatial_bias": normal_values(splits[2], (C,), 0.5, 3.0, ((0, 4),), jnp.float32),
        "norm_gain": jnp.clip(1.0 + 0.18 * jax.random.normal(splits[3], (C,), jnp.float32), 0.1, 1.9),
        "norm_shift": normal_values(splits[4], (C,), 0.5, 3.0, ((0, 4),), jnp.float32),
        "temporal_weight": normal_values(splits[5], (3, C, C), (3 * C) ** -0.5, 0.09375, ((1, 4),)),
        "temporal_bias": normal_values(splits[6], (C,), 0.5, 3.0, (), jnp.float32),
        "token_gain": jnp.clip(1.0 + 0.18 * jax.random.normal(splits[7], (C,), jnp.float32), 0.1, 1.9),
        "query_weight": draw_query_weight(jax.random.fold_in(splits[12], 71), part),
        "key_weight": draw_key_weight(jax.random.fold_in(splits[12], 71), part),
        "value_weight": normal_values(splits[10], (C, HEADS * HD), C ** -0.5, 0.15625, ((1, 4),)),
        "output_weight": normal_values(splits[11], (HEADS * HD, C), (HEADS * HD) ** -0.5, 0.1875, ((0, 4),)),
    }


def conv_plane(field, weight, bias):
    rows_n, frames_n, cols_n, chans = field.shape
    padded = jnp.pad(field, ((1, 1), (0, 0), (1, 1), (0, 0)))
    total = jnp.zeros((rows_n * frames_n * cols_n, weight.shape[3]), jnp.float32)
    for row_off in range(3):
        for col_off in range(3):
            window = padded[row_off:row_off + rows_n, :, col_off:col_off + cols_n, :].reshape(-1, chans)
            total = total + jnp.dot(window, weight[row_off, col_off], preferred_element_type=jnp.float32)
    return total.reshape(rows_n, frames_n, cols_n, -1) + bias

def head_attention(query, keys, values):
    block = math.gcd(query.shape[0], 1024)
    scale = 1.0 / math.sqrt(HD)

    def one_block(query_block):
        scores = jnp.dot(query_block, keys.T, preferred_element_type=jnp.float32) * scale
        peak = lax.optimization_barrier(jnp.max(scores, axis=-1, keepdims=True))
        weights = jnp.exp(scores - peak)
        denominator = lax.optimization_barrier(jnp.sum(weights, axis=-1, keepdims=True))
        return jnp.dot(weights.astype(jnp.bfloat16), values, preferred_element_type=jnp.float32) / denominator
    return lax.map(one_block, query.reshape(-1, block, HD)).reshape(-1, HD)

def reference(latents, spatial_weight, spatial_bias, norm_gain, norm_shift, temporal_weight, temporal_bias, token_gain, query_weight, key_weight, value_weight, output_weight):
    spatial = conv_plane(latents, spatial_weight, spatial_bias)
    grouped = spatial.reshape(LAT_H, FRAMES, LAT_W, NORM_GROUPS, -1)
    group_mean = lax.optimization_barrier(jnp.mean(grouped, axis=(0, 2, 4), keepdims=True))
    centred = grouped - group_mean
    group_var = lax.optimization_barrier(jnp.mean(centred * centred, axis=(0, 2, 4), keepdims=True))
    scaled = (centred / jnp.sqrt(group_var + 1e-05)).reshape(LAT_H, FRAMES, LAT_W, C) * norm_gain + norm_shift
    activated = jax.nn.silu(scaled).astype(jnp.bfloat16)
    rim = jnp.pad(activated, ((0, 0), (1, 1), (0, 0), (0, 0)))
    temporal = jnp.zeros((LAT_H * FRAMES * LAT_W, C), jnp.float32)
    for lag_index in range(3):
        window = rim[:, lag_index:lag_index + FRAMES].reshape(-1, C)
        temporal = temporal + jnp.dot(window, temporal_weight[lag_index], preferred_element_type=jnp.float32)
    temporal = temporal.reshape(LAT_H, FRAMES, LAT_W, C) + temporal_bias
    hidden = (latents.astype(jnp.float32) + temporal).astype(jnp.bfloat16)
    flat = hidden.reshape(-1, C).astype(jnp.float32)
    token_mean = lax.optimization_barrier(jnp.mean(flat, axis=-1, keepdims=True))
    shifted = flat - token_mean
    token_var = lax.optimization_barrier(jnp.mean(shifted * shifted, axis=-1, keepdims=True))
    normed = (shifted / jnp.sqrt(token_var + 1e-05) * token_gain).astype(jnp.bfloat16)
    queries = jnp.dot(normed, query_weight, preferred_element_type=jnp.float32).astype(jnp.bfloat16)
    keys = jnp.dot(normed, key_weight, preferred_element_type=jnp.float32).astype(jnp.bfloat16)
    values = jnp.dot(normed, value_weight, preferred_element_type=jnp.float32).astype(jnp.bfloat16)

    def by_head(array):
        return array.reshape(TOKENS, HEADS, HD).transpose(1, 0, 2)
    per_head = lax.map(lambda trio: head_attention(trio[0], trio[1], trio[2]), (by_head(queries), by_head(keys), by_head(values)))
    attended = per_head.transpose(1, 0, 2).reshape(TOKENS, HEADS * HD).astype(jnp.bfloat16)
    projected = jnp.dot(attended, output_weight, preferred_element_type=jnp.float32)
    denoised = hidden.reshape(-1, C).astype(jnp.float32) + projected
    return denoised.reshape(LAT_H, FRAMES, LAT_W, C).astype(jnp.bfloat16)
```

```python
import functools
import math

import jax
import jax.numpy as jnp
from jax import lax
from jax.experimental import pallas as pl
from jax.experimental.pallas import tpu as pltpu
from jax.sharding import PartitionSpec as P

HD = 64
NORM_GROUPS = 32


def padded_2(array, sides, width):
    for axis, dim in sides:
        peers, length = (lax.axis_size(axis), array.shape[dim])
        up = [(i, (i + 1) % peers) for i in range(peers - 1)]
        down = [(j, i) for i, j in up]
        last = lax.slice_in_dim(array, length - width, length, axis=dim)
        leading = lax.slice_in_dim(array, 0, width, axis=dim)
        before = lax.ppermute(last, axis, up)
        after = lax.ppermute(leading, axis, down)
        array = jnp.concatenate([before, array, after], axis=dim)
    return array


def shifted_2(value, axis, steps):
    count = lax.axis_size(axis)
    pairs = [(source, (source + steps) % count) for source in range(count)]
    return lax.ppermute(value, axis, pairs)


def conv_plane(field, weight, bias):
    rows_n, frames_n, cols_n, chans = field.shape
    padded = jnp.pad(field, ((1, 1), (0, 0), (1, 1), (0, 0)))
    total = jnp.zeros((rows_n * frames_n * cols_n, weight.shape[3]), jnp.float32)
    for row_off in range(3):
        for col_off in range(3):
            window = padded[row_off : row_off + rows_n, :, col_off : col_off + cols_n, :].reshape(
                -1, chans
            )
            total = total + jnp.dot(
                window, weight[row_off, col_off], preferred_element_type=jnp.float32
            )
    return total.reshape(rows_n, frames_n, cols_n, -1) + bias


def layer_norm(field, token_gain):
    flat = field.astype(jnp.float32)
    token_mean = jnp.mean(flat, axis=-1, keepdims=True)
    shifted = flat - token_mean
    token_var = jnp.mean(shifted * shifted, axis=-1, keepdims=True)
    return (shifted / jnp.sqrt(token_var + 1e-05) * token_gain).astype(jnp.bfloat16)


def attend(queries, carried, keys, values):
    block = queries.shape[0]
    head_count = queries.shape[1]
    block_count = keys.shape[0] // block
    key_blocks = keys.reshape(block_count, block, head_count, HD)
    value_blocks = values.reshape(block_count, block, head_count, HD)
    scale = 1.0 / math.sqrt(HD)

    def visit_block(state, block_pair):
        running_max, denominator, numerator = state
        key_block, value_block = block_pair
        scores = (
            jnp.einsum("qhd,khd->qhk", queries, key_block, preferred_element_type=jnp.float32)
            * scale
        )
        new_max = jnp.maximum(running_max, jnp.max(scores, axis=-1))
        shrink = jnp.exp(running_max - new_max)
        weights = jnp.exp(scores - new_max[..., None])
        denominator = denominator * shrink + jnp.sum(weights, axis=-1)
        numerator = numerator * shrink[..., None] + jnp.einsum(
            "qhk,khd->qhd",
            weights.astype(jnp.bfloat16),
            value_block,
            preferred_element_type=jnp.float32,
        )
        return ((new_max, denominator, numerator), None)

    result, _ = lax.scan(visit_block, carried, (key_blocks, value_blocks))
    return result


def body(
    latents,
    spatial_weight,
    spatial_bias,
    norm_gain,
    norm_shift,
    temporal_weight,
    temporal_bias,
    token_gain,
    query_weight,
    key_weight,
    value_weight,
    output_weight,
):
    row_count, frame_count, width_cells, channels = latents.shape
    plane = lax.all_gather(latents, "rows", axis=0, tiled=True)
    plane_rows = plane.shape[0]
    local_out = spatial_weight.shape[3]
    spatial = conv_plane(plane, spatial_weight, spatial_bias)
    local_groups = NORM_GROUPS // lax.axis_size("rows")
    grouped = spatial.reshape(plane_rows, frame_count, width_cells, local_groups, -1)
    group_mean = jnp.mean(grouped, axis=(0, 2, 4), keepdims=True)
    centred = grouped - group_mean
    group_var = jnp.mean(centred * centred, axis=(0, 2, 4), keepdims=True)
    scaled = (centred / jnp.sqrt(group_var + 1e-05)).reshape(
        plane_rows, frame_count, width_cells, local_out
    ) * norm_gain + norm_shift
    activated = jax.nn.silu(scaled).astype(jnp.bfloat16)
    rim = padded_2(activated, (("frames", 1),), 1)
    row_total = row_count * lax.axis_size("rows")
    row_piece = rim
    total = jnp.zeros((row_total * frame_count * width_cells, channels), jnp.float32)
    for lag_index in range(3):
        window = row_piece[:, lag_index : lag_index + frame_count].reshape(-1, local_out)
        total = total + jnp.dot(
            window, temporal_weight[lag_index], preferred_element_type=jnp.float32
        )
    temporal = lax.psum_scatter(
        total.reshape(row_total, frame_count, width_cells, channels).astype(jnp.bfloat16),
        "rows",
        scatter_dimension=0,
        tiled=True,
    ).astype(jnp.float32)
    hidden = (latents.astype(jnp.float32) + temporal + temporal_bias).astype(jnp.bfloat16)
    normed_all = lax.all_gather(layer_norm(hidden, token_gain), "rows", axis=0, tiled=True)
    flat = normed_all.reshape(-1, channels)
    head_cols = query_weight.shape[1]
    head_count = head_cols // HD
    token_count = flat.shape[0]
    queries = jnp.dot(flat, query_weight, preferred_element_type=jnp.float32).astype(jnp.bfloat16)
    keys = jnp.dot(flat, key_weight, preferred_element_type=jnp.float32).astype(jnp.bfloat16)
    values = jnp.dot(flat, value_weight, preferred_element_type=jnp.float32).astype(jnp.bfloat16)
    start_state = (
        jnp.full((token_count, head_count), -1e30, jnp.float32),
        jnp.zeros((token_count, head_count), jnp.float32),
        jnp.zeros((token_count, head_count, HD), jnp.float32),
    )
    local_keys = keys.reshape(token_count, head_count, HD)
    local_values = values.reshape(token_count, head_count, HD)

    def travel(turn, state):
        query_moving, running_max, denominator, numerator = state
        running_max, denominator, numerator = attend(
            query_moving, (running_max, denominator, numerator), local_keys, local_values
        )
        return (
            shifted_2(query_moving, "frames", 1),
            shifted_2(running_max.astype(jnp.bfloat16), "frames", 1).astype(running_max.dtype),
            shifted_2(denominator.astype(jnp.bfloat16), "frames", 1).astype(denominator.dtype),
            shifted_2(numerator.astype(jnp.bfloat16), "frames", 1).astype(numerator.dtype),
        )

    start_moving = queries.reshape(token_count, head_count, HD)
    final = lax.fori_loop(0, lax.axis_size("frames"), travel, (start_moving,) + start_state)
    denominator, numerator = (final[2], final[3])
    attended = (
        (numerator / denominator[..., None])
        .astype(jnp.bfloat16)
        .reshape(plane_rows, frame_count, width_cells, head_cols)
    )
    row_piece = attended
    mixed = lax.psum_scatter(
        jnp.dot(row_piece.reshape(-1, head_cols), output_weight, preferred_element_type=jnp.float32)
        .reshape(row_count * lax.axis_size("rows"), frame_count, width_cells, channels)
        .astype(jnp.bfloat16),
        "rows",
        scatter_dimension=0,
        tiled=True,
    ).astype(jnp.float32)
    return (hidden.astype(jnp.float32) + mixed).astype(jnp.bfloat16)


MESH = pl.DeviceIdType.MESH
DMA = pltpu.SemaphoreType.DMA
VMEM_SPEC = pl.BlockSpec(memory_space=pltpu.VMEM)
ANY_SPEC = pl.BlockSpec(memory_space=pl.ANY)
BF16 = jnp.bfloat16
F32 = jnp.float32
VMEM_LIMIT = 40 << 20
PARTS = 2


def remote(src, dst, send, recv, axis, peer):
    return pltpu.make_async_remote_copy(
        src_ref=src,
        dst_ref=dst,
        send_sem=send,
        recv_sem=recv,
        device_id={axis: peer},
        device_id_type=MESH,
    )


def greet(barrier, axis, peer):
    pl.semaphore_signal(barrier, inc=1, device_id={axis: peer}, device_id_type=MESH)


class Gather:
    def __init__(self, block, out, send, recv):
        me = lax.axis_index("rows")
        near, far = me ^ 1, me ^ 2
        step = block.shape[0] // PARTS
        self.far, self.onward = [], []
        for part in range(PARTS):
            piece = pl.ds(part * step, step)
            self.far.append(
                remote(
                    block.at[piece],
                    out.at[me, piece],
                    send.at[part],
                    recv.at[part],
                    "rows",
                    far,
                )
            )
            self.onward.append(
                remote(
                    out.at[far, piece],
                    out.at[far, piece],
                    send.at[PARTS + part],
                    recv.at[PARTS + part],
                    "rows",
                    near,
                )
            )
        self.near = remote(
            block, out.at[me], send.at[2 * PARTS], recv.at[2 * PARTS], "rows", near
        )

    def start(self):
        for copy in self.far:
            copy.start()
        self.near.start()

    def finish(self):
        for copy, onward in zip(self.far, self.onward):
            copy.wait_recv()
            onward.start()
        for copy in self.far:
            copy.wait_send()
        self.near.wait()
        for onward in self.onward:
            onward.wait()


def reduce_rows(term, sent, got_near, got_far, send, recv):
    me = lax.axis_index("rows")
    near, far = me ^ 1, me ^ 2
    copies = []
    for slot, block in enumerate((far ^ 1, near)):
        sent[slot] = term(block).astype(BF16)
        copy = remote(
            sent.at[slot], got_near.at[slot], send.at[slot], recv.at[slot], "rows", near
        )
        copy.start()
        copies.append(copy)
    mine = term(far)
    copies[0].wait_recv()
    sent[2] = (mine + got_near[0].astype(F32)).astype(BF16)
    across = remote(sent.at[2], got_far, send.at[2], recv.at[2], "rows", far)
    across.start()
    mine = term(me)
    copies[1].wait_recv()
    mine = mine + got_near[1].astype(F32)
    across.wait_recv()
    total = mine + got_far[...].astype(F32)
    for copy in copies + [across]:
        copy.wait_send()
    return total


def gather_kernel(x_ref, out_ref, send, recv):
    me = lax.axis_index("rows")
    barrier = pltpu.get_barrier_semaphore()
    greet(barrier, "rows", me ^ 1)
    greet(barrier, "rows", me ^ 2)
    pl.semaphore_wait(barrier, 2)
    gather = Gather(x_ref, out_ref, send, recv)
    gather.start()
    out_ref[me] = x_ref[...]
    gather.finish()


def temporal_kernel(
    frames,
    act,
    weight_hbm,
    latents,
    bias,
    gain,
    hidden_ref,
    normed_all,
    weight,
    halo,
    sent,
    got_near,
    got_far,
    normed,
    load_sem,
    halo_send,
    halo_recv,
    sum_send,
    sum_recv,
    gat_send,
    gat_recv,
):
    load = pltpu.make_async_copy(weight_hbm, weight, load_sem)
    load.start()
    me = lax.axis_index("rows")
    frame = lax.axis_index("frames")
    has_prev, has_next = frame > 0, frame < frames - 1
    prev = jnp.maximum(frame - 1, 0)
    later = jnp.minimum(frame + 1, frames - 1)
    barrier = pltpu.get_barrier_semaphore()
    greet(barrier, "rows", me ^ 1)
    greet(barrier, "rows", me ^ 2)

    @pl.when(has_prev)
    def _():
        greet(barrier, "frames", prev)

    @pl.when(has_next)
    def _():
        greet(barrier, "frames", later)

    pl.semaphore_wait(barrier, 2 + has_prev.astype(jnp.int32) + has_next.astype(jnp.int32))

    up = remote(act, halo.at[0], halo_send.at[0], halo_recv.at[0], "frames", later)
    down = remote(act, halo.at[1], halo_send.at[1], halo_recv.at[1], "frames", prev)

    @pl.when(has_next)
    def _():
        up.start()

    @pl.when(has_prev)
    def _():
        down.start()

    load.wait()

    @pl.when(has_prev)
    def _():
        up.wait_recv()

    @pl.when(jnp.logical_not(has_prev))
    def _():
        halo[0] = jnp.zeros(halo.shape[1:], halo.dtype)

    @pl.when(has_next)
    def _():
        down.wait_recv()

    @pl.when(jnp.logical_not(has_next))
    def _():
        halo[1] = jnp.zeros(halo.shape[1:], halo.dtype)

    size = latents.shape[0]

    def term(block):
        rows = pl.ds(pl.multiple_of(block * size, size), size)
        total = jnp.dot(act[rows, :], weight[1], preferred_element_type=F32)
        total += jnp.dot(halo[0, rows, :], weight[0], preferred_element_type=F32)
        total += jnp.dot(halo[1, rows, :], weight[2], preferred_element_type=F32)
        return total

    temporal = reduce_rows(term, sent, got_near, got_far, sum_send, sum_recv)
    hidden = (latents[...].astype(F32) + temporal + bias[...]).astype(BF16)
    hidden_ref[...] = hidden
    flat = hidden.astype(F32)
    shifted = flat - jnp.mean(flat, axis=-1, keepdims=True)
    var = jnp.mean(shifted * shifted, axis=-1, keepdims=True)
    value = (shifted / jnp.sqrt(var + 1e-05) * gain[...]).astype(BF16)
    normed[...] = value
    gather = Gather(normed, normed_all, gat_send, gat_recv)
    gather.start()
    normed_all[me] = value
    gather.finish()

    @pl.when(has_next)
    def _():
        up.wait_send()

    @pl.when(has_prev)
    def _():
        down.wait_send()


def attention_kernel(
    frames,
    q_ref,
    k_ref,
    v_ref,
    weight_hbm,
    hidden,
    out_ref,
    weight,
    got,
    keys,
    values,
    done,
    back,
    att,
    sent,
    got_near,
    got_far,
    load_sem,
    in_send,
    in_recv,
    out_send,
    out_recv,
    sum_send,
    sum_recv,
):
    load = pltpu.make_async_copy(weight_hbm, weight, load_sem)
    load.start()
    me = lax.axis_index("rows")
    frame = lax.axis_index("frames")
    barrier = pltpu.get_barrier_semaphore()
    greet(barrier, "rows", me ^ 1)
    greet(barrier, "rows", me ^ 2)
    for turn in range(1, frames):
        greet(barrier, "frames", lax.rem(frame + turn, frames))
    pl.semaphore_wait(barrier, frames + 1)
    copies = []
    for kind, ref in ((0, k_ref), (1, q_ref), (2, v_ref)):
        for turn in range(1, frames):
            peer = lax.rem(frame + turn, frames)
            copy = remote(
                ref.at[peer],
                got.at[kind, frame],
                in_send.at[kind, turn],
                in_recv.at[kind, turn],
                "frames",
                peer,
            )
            copy.start()
            copies.append(copy)
        got[kind, frame] = ref[frame]
    for copy in copies:
        copy.wait_recv()
    width, tokens = got.shape[2], got.shape[3]
    for source in range(frames):
        span = slice(source * tokens, (source + 1) * tokens)
        keys[span, :] = got[0, source].astype(F32).T.astype(BF16)
        values[:, span] = got[2, source]
    scale = 1.0 / math.sqrt(HD)
    returns = []
    for turn in range(1, frames + 1):
        peer = lax.rem(frame + turn, frames)
        for head in range(width // HD):
            cols = slice(head * HD, (head + 1) * HD)
            query = got[1, peer, cols, :]
            scores = jnp.dot(keys[:, cols], query, preferred_element_type=F32) * scale
            weights = jnp.exp(scores - jnp.max(scores, axis=0, keepdims=True))
            denominator = jnp.sum(weights, axis=0, keepdims=True)
            numerator = jnp.dot(
                values[cols, :], weights.astype(BF16), preferred_element_type=F32
            )
            done[peer, cols, :] = (numerator / denominator).astype(BF16)
        if turn < frames:
            copy = remote(
                done.at[peer],
                back.at[frame],
                out_send.at[turn],
                out_recv.at[turn],
                "frames",
                peer,
            )
            copy.start()
            returns.append(copy)
    back[frame] = done[frame]
    load.wait()
    for copy in returns:
        copy.wait_recv()
    for source in range(frames):
        att[:, source * width : (source + 1) * width] = (
            back[source].astype(F32).T.astype(BF16)
        )
    size = hidden.shape[0]

    def term(block):
        rows = pl.ds(pl.multiple_of(block * size, size), size)
        return jnp.dot(att[rows, :], weight[...], preferred_element_type=F32)

    mixed = reduce_rows(term, sent, got_near, got_far, sum_send, sum_recv)
    out_ref[...] = (hidden[...].astype(F32) + mixed).astype(BF16)
    for copy in copies + returns:
        copy.wait_send()


def params(number):
    return pltpu.CompilerParams(
        collective_id=number, has_side_effects=True, vmem_limit_bytes=VMEM_LIMIT
    )


def sum_scratch(size, channels):
    return [
        pltpu.VMEM((3, size, channels), BF16),
        pltpu.VMEM((2, size, channels), BF16),
        pltpu.VMEM((size, channels), BF16),
    ]


def gather_rows(block):
    peers = lax.axis_size("rows")
    return pl.pallas_call(
        gather_kernel,
        out_shape=jax.ShapeDtypeStruct((peers,) + block.shape, block.dtype),
        in_specs=[VMEM_SPEC],
        out_specs=VMEM_SPEC,
        scratch_shapes=[DMA((2 * PARTS + 1,)), DMA((2 * PARTS + 1,))],
        compiler_params=params(0),
    )(block)


def temporal_normed(act, weight, latents, bias, gain):
    peers, frames = lax.axis_size("rows"), lax.axis_size("frames")
    size, channels = latents.shape
    return pl.pallas_call(
        functools.partial(temporal_kernel, frames),
        out_shape=(
            jax.ShapeDtypeStruct((size, channels), BF16),
            jax.ShapeDtypeStruct((peers, size, channels), BF16),
        ),
        in_specs=[VMEM_SPEC, ANY_SPEC] + [VMEM_SPEC] * 3,
        out_specs=(VMEM_SPEC, VMEM_SPEC),
        scratch_shapes=[
            pltpu.VMEM(weight.shape, BF16),
            pltpu.VMEM((2,) + act.shape, BF16),
            *sum_scratch(size, channels),
            pltpu.VMEM((size, channels), BF16),
            DMA,
            DMA((2,)),
            DMA((2,)),
            DMA((3,)),
            DMA((3,)),
            DMA((2 * PARTS + 1,)),
            DMA((2 * PARTS + 1,)),
        ],
        compiler_params=params(1),
    )(act, weight, latents, bias.reshape(1, -1), gain.reshape(1, -1))


def attended_mixed(queries, keys, values, weight, hidden):
    frames = lax.axis_size("frames")
    size, channels = hidden.shape
    _, width, tokens = queries.shape
    return pl.pallas_call(
        functools.partial(attention_kernel, frames),
        out_shape=jax.ShapeDtypeStruct((size, channels), BF16),
        in_specs=[VMEM_SPEC] * 3 + [ANY_SPEC, VMEM_SPEC],
        out_specs=VMEM_SPEC,
        scratch_shapes=[
            pltpu.VMEM(weight.shape, BF16),
            pltpu.VMEM((3, frames, width, tokens), BF16),
            pltpu.VMEM((frames * tokens, width), BF16),
            pltpu.VMEM((width, frames * tokens), BF16),
            pltpu.VMEM((frames, width, tokens), BF16),
            pltpu.VMEM((frames, width, tokens), BF16),
            pltpu.VMEM((tokens, frames * width), BF16),
            *sum_scratch(size, channels),
            DMA,
            DMA((3, frames)),
            DMA((3, frames)),
            DMA((frames,)),
            DMA((frames,)),
            DMA((3,)),
            DMA((3,)),
        ],
        compiler_params=params(2),
    )(queries, keys, values, weight, hidden)


def activate(plane, spatial_weight, spatial_bias, norm_gain, norm_shift):
    plane_rows, frame_count, width_cells, _ = plane.shape
    local_out = spatial_weight.shape[3]
    spatial = conv_plane(plane, spatial_weight, spatial_bias)
    local_groups = NORM_GROUPS // lax.axis_size("rows")
    grouped = spatial.reshape(plane_rows, frame_count, width_cells, local_groups, -1)
    group_mean = jnp.mean(grouped, axis=(0, 2, 4), keepdims=True)
    centred = grouped - group_mean
    group_var = jnp.mean(centred * centred, axis=(0, 2, 4), keepdims=True)
    scaled = (centred / jnp.sqrt(group_var + 1e-05)).reshape(
        plane_rows, frame_count, width_cells, local_out
    ) * norm_gain + norm_shift
    return jax.nn.silu(scaled).astype(jnp.bfloat16)


def body_fast(
    latents,
    spatial_weight,
    spatial_bias,
    norm_gain,
    norm_shift,
    temporal_weight,
    temporal_bias,
    token_gain,
    query_weight,
    key_weight,
    value_weight,
    output_weight,
):
    row_count, frame_count, width_cells, channels = latents.shape
    peers, frames = lax.axis_size("rows"), lax.axis_size("frames")
    block = latents.reshape(-1, channels)
    plane = gather_rows(block).reshape(peers * row_count, frame_count, width_cells, channels)
    activated = activate(plane, spatial_weight, spatial_bias, norm_gain, norm_shift)
    hidden, normed_all = temporal_normed(
        activated.reshape(-1, activated.shape[3]),
        temporal_weight,
        block,
        temporal_bias,
        token_gain,
    )
    flat = normed_all.reshape(-1, channels)

    def project(weight):
        cols = lax.dot_general(
            weight, flat, (((0,), (1,)), ((), ())), preferred_element_type=F32
        ).astype(BF16)
        return cols.reshape(frames, -1, flat.shape[0])

    denoised = attended_mixed(
        project(query_weight), project(key_weight), project(value_weight), output_weight, hidden
    )
    return denoised.reshape(latents.shape)


def fits(mesh):
    def choose(*args):
        latents, query_weight = args[0], args[8]
        peers, frames = mesh.shape["rows"], mesh.shape["frames"]
        heads = query_weight.shape[1] // HD
        tokens = latents.shape[0] * latents.shape[1] * latents.shape[2] * peers
        fast = (
            peers == 4
            and latents.shape[1] == 1
            and heads % frames == 0
            and tokens % 128 == 0
        )
        return (body_fast if fast else body)(*args)

    return choose


def solution(mesh):
    in_specs = (
        P("rows", ("groups", "frames"), None, None),
        P(None, None, None, "rows"),
        P("rows"),
        P("rows"),
        P("rows"),
        P(None, "rows", None),
        P(),
        P(),
        P(None, "rows"),
        P(None, "rows"),
        P(None, "rows"),
        P("rows", None),
    )
    out_specs = P("rows", ("groups", "frames"), None, None)
    return jax.shard_map(
        fits(mesh), mesh=mesh, in_specs=in_specs, out_specs=out_specs, check_vma=False
    )
```

```python
import functools
import math

import jax
import jax.numpy as jnp
from jax import lax
from jax.experimental import pallas as pl
from jax.experimental.pallas import tpu as pltpu
from jax.sharding import PartitionSpec as P

HD = 64
NORM_GROUPS = 32


def padded_2(array, sides, width):
    for axis, dim in sides:
        peers, length = (lax.axis_size(axis), array.shape[dim])
        up = [(i, (i + 1) % peers) for i in range(peers - 1)]
        down = [(j, i) for i, j in up]
        last = lax.slice_in_dim(array, length - width, length, axis=dim)
        leading = lax.slice_in_dim(array, 0, width, axis=dim)
        before = lax.ppermute(last, axis, up)
        after = lax.ppermute(leading, axis, down)
        array = jnp.concatenate([before, array, after], axis=dim)
    return array


def shifted_2(value, axis, steps):
    count = lax.axis_size(axis)
    pairs = [(source, (source + steps) % count) for source in range(count)]
    return lax.ppermute(value, axis, pairs)


def conv_plane(field, weight, bias):
    rows_n, frames_n, cols_n, chans = field.shape
    padded = jnp.pad(field, ((1, 1), (0, 0), (1, 1), (0, 0)))
    total = jnp.zeros((rows_n * frames_n * cols_n, weight.shape[3]), jnp.float32)
    for row_off in range(3):
        for col_off in range(3):
            window = padded[row_off : row_off + rows_n, :, col_off : col_off + cols_n, :].reshape(
                -1, chans
            )
            total = total + jnp.dot(
                window, weight[row_off, col_off], preferred_element_type=jnp.float32
            )
    return total.reshape(rows_n, frames_n, cols_n, -1) + bias


def layer_norm(field, token_gain):
    flat = field.astype(jnp.float32)
    token_mean = jnp.mean(flat, axis=-1, keepdims=True)
    shifted = flat - token_mean
    token_var = jnp.mean(shifted * shifted, axis=-1, keepdims=True)
    return (shifted / jnp.sqrt(token_var + 1e-05) * token_gain).astype(jnp.bfloat16)


def attend(queries, carried, keys, values):
    block = queries.shape[0]
    head_count = queries.shape[1]
    block_count = keys.shape[0] // block
    key_blocks = keys.reshape(block_count, block, head_count, HD)
    value_blocks = values.reshape(block_count, block, head_count, HD)
    scale = 1.0 / math.sqrt(HD)

    def visit_block(state, block_pair):
        running_max, denominator, numerator = state
        key_block, value_block = block_pair
        scores = (
            jnp.einsum("qhd,khd->qhk", queries, key_block, preferred_element_type=jnp.float32)
            * scale
        )
        new_max = jnp.maximum(running_max, jnp.max(scores, axis=-1))
        shrink = jnp.exp(running_max - new_max)
        weights = jnp.exp(scores - new_max[..., None])
        denominator = denominator * shrink + jnp.sum(weights, axis=-1)
        numerator = numerator * shrink[..., None] + jnp.einsum(
            "qhk,khd->qhd",
            weights.astype(jnp.bfloat16),
            value_block,
            preferred_element_type=jnp.float32,
        )
        return ((new_max, denominator, numerator), None)

    result, _ = lax.scan(visit_block, carried, (key_blocks, value_blocks))
    return result


def body(
    latents,
    spatial_weight,
    spatial_bias,
    norm_gain,
    norm_shift,
    temporal_weight,
    temporal_bias,
    token_gain,
    query_weight,
    key_weight,
    value_weight,
    output_weight,
):
    row_count, frame_count, width_cells, channels = latents.shape
    plane = lax.all_gather(latents, "rows", axis=0, tiled=True)
    plane_rows = plane.shape[0]
    local_out = spatial_weight.shape[3]
    spatial = conv_plane(plane, spatial_weight, spatial_bias)
    local_groups = NORM_GROUPS // lax.axis_size("rows")
    grouped = spatial.reshape(plane_rows, frame_count, width_cells, local_groups, -1)
    group_mean = jnp.mean(grouped, axis=(0, 2, 4), keepdims=True)
    centred = grouped - group_mean
    group_var = jnp.mean(centred * centred, axis=(0, 2, 4), keepdims=True)
    scaled = (centred / jnp.sqrt(group_var + 1e-05)).reshape(
        plane_rows, frame_count, width_cells, local_out
    ) * norm_gain + norm_shift
    activated = jax.nn.silu(scaled).astype(jnp.bfloat16)
    rim = padded_2(activated, (("frames", 1),), 1)
    row_total = row_count * lax.axis_size("rows")
    row_piece = rim
    total = jnp.zeros((row_total * frame_count * width_cells, channels), jnp.float32)
    for lag_index in range(3):
        window = row_piece[:, lag_index : lag_index + frame_count].reshape(-1, local_out)
        total = total + jnp.dot(
            window, temporal_weight[lag_index], preferred_element_type=jnp.float32
        )
    temporal = lax.psum_scatter(
        total.reshape(row_total, frame_count, width_cells, channels).astype(jnp.bfloat16),
        "rows",
        scatter_dimension=0,
        tiled=True,
    ).astype(jnp.float32)
    hidden = (latents.astype(jnp.float32) + temporal + temporal_bias).astype(jnp.bfloat16)
    normed_all = lax.all_gather(layer_norm(hidden, token_gain), "rows", axis=0, tiled=True)
    flat = normed_all.reshape(-1, channels)
    head_cols = query_weight.shape[1]
    head_count = head_cols // HD
    token_count = flat.shape[0]
    queries = jnp.dot(flat, query_weight, preferred_element_type=jnp.float32).astype(jnp.bfloat16)
    keys = jnp.dot(flat, key_weight, preferred_element_type=jnp.float32).astype(jnp.bfloat16)
    values = jnp.dot(flat, value_weight, preferred_element_type=jnp.float32).astype(jnp.bfloat16)
    start_state = (
        jnp.full((token_count, head_count), -1e30, jnp.float32),
        jnp.zeros((token_count, head_count), jnp.float32),
        jnp.zeros((token_count, head_count, HD), jnp.float32),
    )
    local_keys = keys.reshape(token_count, head_count, HD)
    local_values = values.reshape(token_count, head_count, HD)

    def travel(turn, state):
        query_moving, running_max, denominator, numerator = state
        running_max, denominator, numerator = attend(
            query_moving, (running_max, denominator, numerator), local_keys, local_values
        )
        return (
            shifted_2(query_moving, "frames", 1),
            shifted_2(running_max.astype(jnp.bfloat16), "frames", 1).astype(running_max.dtype),
            shifted_2(denominator.astype(jnp.bfloat16), "frames", 1).astype(denominator.dtype),
            shifted_2(numerator.astype(jnp.bfloat16), "frames", 1).astype(numerator.dtype),
        )

    start_moving = queries.reshape(token_count, head_count, HD)
    final = lax.fori_loop(0, lax.axis_size("frames"), travel, (start_moving,) + start_state)
    denominator, numerator = (final[2], final[3])
    attended = (
        (numerator / denominator[..., None])
        .astype(jnp.bfloat16)
        .reshape(plane_rows, frame_count, width_cells, head_cols)
    )
    row_piece = attended
    mixed = lax.psum_scatter(
        jnp.dot(row_piece.reshape(-1, head_cols), output_weight, preferred_element_type=jnp.float32)
        .reshape(row_count * lax.axis_size("rows"), frame_count, width_cells, channels)
        .astype(jnp.bfloat16),
        "rows",
        scatter_dimension=0,
        tiled=True,
    ).astype(jnp.float32)
    return (hidden.astype(jnp.float32) + mixed).astype(jnp.bfloat16)


MESH = pl.DeviceIdType.MESH
DMA = pltpu.SemaphoreType.DMA
VMEM_SPEC = pl.BlockSpec(memory_space=pltpu.VMEM)
ANY_SPEC = pl.BlockSpec(memory_space=pl.ANY)
BF16 = jnp.bfloat16
F32 = jnp.float32
VMEM_LIMIT = 56 << 20
PARTS = 2


def remote(src, dst, send, recv, axis, peer):
    return pltpu.make_async_remote_copy(
        src_ref=src,
        dst_ref=dst,
        send_sem=send,
        recv_sem=recv,
        device_id={axis: peer},
        device_id_type=MESH,
    )


def greet(barrier, axis, peer):
    pl.semaphore_signal(barrier, inc=1, device_id={axis: peer}, device_id_type=MESH)


class Gather:
    def __init__(self, block, out, send, recv):
        me = lax.axis_index("rows")
        near, far = me ^ 1, me ^ 2
        step = block.shape[0] // PARTS
        self.far, self.onward = [], []
        for part in range(PARTS):
            piece = pl.ds(part * step, step)
            self.far.append(
                remote(
                    block.at[piece],
                    out.at[me, piece],
                    send.at[part],
                    recv.at[part],
                    "rows",
                    far,
                )
            )
            self.onward.append(
                remote(
                    out.at[far, piece],
                    out.at[far, piece],
                    send.at[PARTS + part],
                    recv.at[PARTS + part],
                    "rows",
                    near,
                )
            )
        self.near = remote(
            block, out.at[me], send.at[2 * PARTS], recv.at[2 * PARTS], "rows", near
        )

    def start(self):
        for copy in self.far:
            copy.start()
        self.near.start()

    def finish(self):
        for copy, onward in zip(self.far, self.onward):
            copy.wait_recv()
            onward.start()
        for copy in self.far:
            copy.wait_send()
        self.near.wait()
        for onward in self.onward:
            onward.wait()


def reduce_rows(term, sent, got_near, got_far, send, recv):
    me = lax.axis_index("rows")
    near, far = me ^ 1, me ^ 2

    def hand(slot, value):
        sent[slot] = value.astype(BF16)
        copy = remote(
            sent.at[slot], got_near.at[slot], send.at[slot], recv.at[slot], "rows", near
        )
        copy.start()
        return copy

    first = hand(0, term(far ^ 1, 0))
    mine = term(far, 1)
    first.wait_recv()
    sent[2] = (mine + got_near[0].astype(F32)).astype(BF16)
    across = remote(sent.at[2], got_far, send.at[2], recv.at[2], "rows", far)
    across.start()
    second = hand(1, term(near, 2))
    mine = term(me, 3)
    second.wait_recv()
    mine = mine + got_near[1].astype(F32)
    across.wait_recv()
    total = mine + got_far[...].astype(F32)
    for copy in (first, second, across):
        copy.wait_send()
    return total


def convolve(plane, shifted, weight, width):
    blocks, size, channels = plane.shape
    tokens = blocks * size
    edge = jnp.zeros((width, channels), BF16)
    column = lax.broadcasted_iota(jnp.int32, (size, channels), 0) % width
    for offset in range(3):
        shifted[offset, :width, :] = edge
        shifted[offset, tokens + width :, :] = edge
    for block in range(blocks):
        rows = slice(width + block * size, width + (block + 1) * size)
        value = plane[block]
        wide = value.astype(F32)
        before = jnp.where(column == 0, 0.0, pltpu.roll(wide, 1, 0))
        after = jnp.where(column == width - 1, 0.0, pltpu.roll(wide, size - 1, 0))
        shifted[0, rows, :] = before.astype(BF16)
        shifted[1, rows, :] = value
        shifted[2, rows, :] = after.astype(BF16)
    total = None
    for row_off in range(3):
        for col_off in range(3):
            window = shifted[col_off, row_off * width : row_off * width + tokens, :]
            part = jnp.dot(window, weight[row_off, col_off], preferred_element_type=F32)
            total = part if total is None else total + part
    return total


def group_norm_silu(spatial, gain, shift, groups):
    tokens, channels = spatial.shape
    per = channels // groups
    lane = lax.broadcasted_iota(jnp.int32, (groups, channels), 1)
    first = lax.broadcasted_iota(jnp.int32, (groups, channels), 0) * per
    member = jnp.logical_and(lane >= first, lane < first + per)

    def group_mean(value):
        column = jnp.sum(value, axis=0, keepdims=True)
        sums = jnp.sum(jnp.where(member, column, 0.0), axis=1, keepdims=True)
        return jnp.sum(jnp.where(member, sums, 0.0), axis=0, keepdims=True) / (tokens * per)

    centred = spatial - group_mean(spatial)
    scale = 1.0 / jnp.sqrt(group_mean(centred * centred) + 1e-05)
    value = centred * scale * gain + shift
    return (value / (1.0 + jnp.exp(-value))).astype(BF16)


def block_kernel(
    frames,
    width_cells,
    groups,
    latents_hbm,
    spatial_hbm,
    spatial_bias,
    norm_gain,
    norm_shift,
    temporal_hbm,
    temporal_bias,
    token_gain,
    query_hbm,
    key_hbm,
    value_hbm,
    output_hbm,
    out_ref,
    latents,
    spatial_w,
    temporal_w,
    project_w,
    output_w,
    plane,
    shifted,
    act,
    halo,
    normed,
    normed_all,
    outgoing,
    got,
    keys,
    values,
    probs,
    done,
    back,
    att,
    sent,
    got_near,
    got_far,
    load_sem,
    lat_send,
    lat_recv,
    halo_send,
    halo_recv,
    gat_send,
    gat_recv,
    in_send,
    in_recv,
    out_send,
    out_recv,
    sum_send,
    sum_recv,
):
    me = lax.axis_index("rows")
    frame = lax.axis_index("frames")
    near, far = me ^ 1, me ^ 2
    loads = []
    for index, (src, dst) in enumerate(
        (
            (latents_hbm, latents),
            (spatial_hbm, spatial_w),
            (temporal_hbm, temporal_w),
            (key_hbm, project_w.at[0]),
            (query_hbm, project_w.at[1]),
            (value_hbm, project_w.at[2]),
            (output_hbm, output_w),
        )
    ):
        load = pltpu.make_async_copy(src, dst, load_sem.at[index])
        load.start()
        loads.append(load)
    barrier = pltpu.get_barrier_semaphore()
    greet(barrier, "rows", near)
    greet(barrier, "rows", far)
    for turn in range(1, frames):
        greet(barrier, "frames", lax.rem(frame + turn, frames))
    pl.semaphore_wait(barrier, frames + 1)

    loads[0].wait()
    gather = Gather(latents, plane, lat_send, lat_recv)
    gather.start()
    plane[me] = latents[...]
    gather.finish()
    loads[1].wait()
    spatial = convolve(plane, shifted, spatial_w, width_cells) + spatial_bias[...]
    act[...] = group_norm_silu(spatial, norm_gain[...], norm_shift[...], groups)

    has_prev, has_next = frame > 0, frame < frames - 1
    prev = jnp.maximum(frame - 1, 0)
    later = jnp.minimum(frame + 1, frames - 1)
    size = latents.shape[0]

    def rows_of(block):
        return pl.ds(pl.multiple_of(block * size, size), size)

    up, down = [], []
    for turn, block in enumerate((far ^ 1, far, near, me)):
        rows = rows_of(block)
        for side, (copies, peer) in enumerate(((up, later), (down, prev))):
            copies.append(
                remote(
                    act.at[rows],
                    halo.at[side, rows],
                    halo_send.at[side, turn],
                    halo_recv.at[side, turn],
                    "frames",
                    peer,
                )
            )

    @pl.when(has_next)
    def _():
        for copy in up:
            copy.start()

    @pl.when(has_prev)
    def _():
        for copy in down:
            copy.start()

    @pl.when(jnp.logical_not(has_prev))
    def _():
        halo[0] = jnp.zeros(halo.shape[1:], halo.dtype)

    @pl.when(jnp.logical_not(has_next))
    def _():
        halo[1] = jnp.zeros(halo.shape[1:], halo.dtype)

    loads[2].wait()

    def temporal_term(block, turn):
        rows = rows_of(block)
        total = jnp.dot(act[rows, :], temporal_w[1], preferred_element_type=F32)

        @pl.when(has_prev)
        def _():
            up[turn].wait_recv()

        @pl.when(has_next)
        def _():
            down[turn].wait_recv()

        total += jnp.dot(halo[0, rows, :], temporal_w[0], preferred_element_type=F32)
        total += jnp.dot(halo[1, rows, :], temporal_w[2], preferred_element_type=F32)
        return total

    temporal = reduce_rows(
        temporal_term, sent.at[0], got_near.at[0], got_far.at[0], sum_send.at[0], sum_recv.at[0]
    )

    @pl.when(has_next)
    def _():
        for copy in up:
            copy.wait_send()

    @pl.when(has_prev)
    def _():
        for copy in down:
            copy.wait_send()

    hidden = (latents[...].astype(F32) + temporal + temporal_bias[...]).astype(BF16)
    flat = hidden.astype(F32)
    centred = flat - jnp.mean(flat, axis=-1, keepdims=True)
    var = jnp.mean(centred * centred, axis=-1, keepdims=True)
    normed[...] = (centred / jnp.sqrt(var + 1e-05) * token_gain[...]).astype(BF16)
    gather = Gather(normed, normed_all, gat_send, gat_recv)
    gather.start()
    normed_all[me] = normed[...]
    gather.finish()

    tokens = act.shape[0]
    width = got.shape[2]
    tokens_in = normed_all[...].reshape(tokens, -1)
    moves = []
    for kind in range(3):
        loads[3 + kind].wait()
        cols = jnp.dot(tokens_in, project_w[kind], preferred_element_type=F32)
        cols = cols.T.astype(BF16)
        for owner in range(frames):
            outgoing[kind, owner] = cols[owner * width : (owner + 1) * width, :]
        batch = []
        for turn in range(1, frames):
            peer = lax.rem(frame + turn, frames)
            copy = remote(
                outgoing.at[kind, peer],
                got.at[kind, frame],
                in_send.at[kind, turn],
                in_recv.at[kind, turn],
                "frames",
                peer,
            )
            copy.start()
            batch.append(copy)
        got[kind, frame] = outgoing[kind, frame]
        moves.append(batch)

    for copy in moves[0]:
        copy.wait_recv()
    for source in range(frames):
        span = slice(source * tokens, (source + 1) * tokens)
        keys[span, :] = got[0, source].astype(F32).T.astype(BF16)
    for copy in moves[1]:
        copy.wait_recv()
    scale = 1.0 / math.sqrt(HD)
    heads = width // HD
    sums = []
    for turn in range(1, frames + 1):
        peer = lax.rem(frame + turn, frames)
        for head in range(heads):
            cols = slice(head * HD, (head + 1) * HD)
            query = got[1, peer, cols, :]
            scores = jnp.dot(keys[:, cols], query, preferred_element_type=F32) * scale
            weights = jnp.exp(scores - jnp.max(scores, axis=0, keepdims=True))
            sums.append(jnp.sum(weights, axis=0, keepdims=True))
            probs[(turn - 1) * heads + head] = weights.astype(BF16)
    for copy in moves[2]:
        copy.wait_recv()
    for source in range(frames):
        values[:, source * tokens : (source + 1) * tokens] = got[2, source]
    returns = []
    for turn in range(1, frames + 1):
        peer = lax.rem(frame + turn, frames)
        for head in range(heads):
            cols = slice(head * HD, (head + 1) * HD)
            place = (turn - 1) * heads + head
            numerator = jnp.dot(values[cols, :], probs[place], preferred_element_type=F32)
            done[peer, cols, :] = (numerator / sums[place]).astype(BF16)
        if turn < frames:
            copy = remote(
                done.at[peer],
                back.at[frame],
                out_send.at[turn],
                out_recv.at[turn],
                "frames",
                peer,
            )
            copy.start()
            returns.append(copy)
    back[frame] = done[frame]
    loads[6].wait()
    for copy in returns:
        copy.wait_recv()
    for source in range(frames):
        att[:, source * width : (source + 1) * width] = (
            back[source].astype(F32).T.astype(BF16)
        )

    def mixed_term(block, turn):
        return jnp.dot(att[rows_of(block), :], output_w[...], preferred_element_type=F32)

    mixed = reduce_rows(
        mixed_term, sent.at[1], got_near.at[1], got_far.at[1], sum_send.at[1], sum_recv.at[1]
    )
    out_ref[...] = (hidden.astype(F32) + mixed).astype(BF16)
    for batch in moves + [returns]:
        for copy in batch:
            copy.wait_send()


def body_fast(
    latents,
    spatial_weight,
    spatial_bias,
    norm_gain,
    norm_shift,
    temporal_weight,
    temporal_bias,
    token_gain,
    query_weight,
    key_weight,
    value_weight,
    output_weight,
):
    channels = latents.shape[3]
    peers, frames = lax.axis_size("rows"), lax.axis_size("frames")
    block = latents.reshape(-1, channels)
    size = block.shape[0]
    tokens = size * peers
    width_cells = latents.shape[2]
    local_out = spatial_weight.shape[3]
    width = query_weight.shape[1] // frames
    heads = width // HD
    links = 2 * PARTS + 1
    denoised = pl.pallas_call(
        functools.partial(block_kernel, frames, width_cells, NORM_GROUPS // peers),
        out_shape=jax.ShapeDtypeStruct(block.shape, BF16),
        in_specs=[ANY_SPEC] * 2
        + [VMEM_SPEC] * 3
        + [ANY_SPEC]
        + [VMEM_SPEC] * 2
        + [ANY_SPEC] * 4,
        out_specs=VMEM_SPEC,
        scratch_shapes=[
            pltpu.VMEM(block.shape, BF16),
            pltpu.VMEM(spatial_weight.shape, BF16),
            pltpu.VMEM(temporal_weight.shape, BF16),
            pltpu.VMEM((3,) + query_weight.shape, BF16),
            pltpu.VMEM(output_weight.shape, BF16),
            pltpu.VMEM((peers,) + block.shape, BF16),
            pltpu.VMEM((3, tokens + 2 * width_cells, channels), BF16),
            pltpu.VMEM((tokens, local_out), BF16),
            pltpu.VMEM((2, tokens, local_out), BF16),
            pltpu.VMEM(block.shape, BF16),
            pltpu.VMEM((peers,) + block.shape, BF16),
            pltpu.VMEM((3, frames, width, tokens), BF16),
            pltpu.VMEM((3, frames, width, tokens), BF16),
            pltpu.VMEM((frames * tokens, width), BF16),
            pltpu.VMEM((width, frames * tokens), BF16),
            pltpu.VMEM((frames * heads, frames * tokens, tokens), BF16),
            pltpu.VMEM((frames, width, tokens), BF16),
            pltpu.VMEM((frames, width, tokens), BF16),
            pltpu.VMEM((tokens, frames * width), BF16),
            pltpu.VMEM((2, 3) + block.shape, BF16),
            pltpu.VMEM((2, 2) + block.shape, BF16),
            pltpu.VMEM((2,) + block.shape, BF16),
            DMA((7,)),
            DMA((links,)),
            DMA((links,)),
            DMA((2, peers)),
            DMA((2, peers)),
            DMA((links,)),
            DMA((links,)),
            DMA((3, frames)),
            DMA((3, frames)),
            DMA((frames,)),
            DMA((frames,)),
            DMA((2, 3)),
            DMA((2, 3)),
        ],
        compiler_params=pltpu.CompilerParams(
            collective_id=0, has_side_effects=True, vmem_limit_bytes=VMEM_LIMIT
        ),
    )(
        block,
        spatial_weight,
        spatial_bias.reshape(1, -1),
        norm_gain.reshape(1, -1),
        norm_shift.reshape(1, -1),
        temporal_weight,
        temporal_bias.reshape(1, -1),
        token_gain.reshape(1, -1),
        query_weight,
        key_weight,
        value_weight,
        output_weight,
    )
    return denoised.reshape(latents.shape)


def fits(mesh):
    def choose(*args):
        latents, query_weight = args[0], args[8]
        peers, frames = mesh.shape["rows"], mesh.shape["frames"]
        heads = query_weight.shape[1] // HD
        tokens = latents.shape[0] * latents.shape[1] * latents.shape[2] * peers
        fast = (
            peers == 4
            and latents.shape[1] == 1
            and heads % frames == 0
            and tokens % 128 == 0
            and latents.shape[2] % 16 == 0
            and latents.shape[0] * latents.shape[2] % (16 * PARTS) == 0
        )
        return (body_fast if fast else body)(*args)

    return choose


def solution(mesh):
    in_specs = (
        P("rows", ("groups", "frames"), None, None),
        P(None, None, None, "rows"),
        P("rows"),
        P("rows"),
        P("rows"),
        P(None, "rows", None),
        P(),
        P(),
        P(None, "rows"),
        P(None, "rows"),
        P(None, "rows"),
        P("rows", None),
    )
    out_specs = P("rows", ("groups", "frames"), None, None)
    return jax.shard_map(
        fits(mesh), mesh=mesh, in_specs=in_specs, out_specs=out_specs, check_vma=False
    )
```

```python
import functools
import math

import jax
import jax.numpy as jnp
from jax import lax
from jax.experimental import pallas as pl
from jax.experimental.pallas import tpu as pltpu
from jax.sharding import PartitionSpec as P

HD = 64
NORM_GROUPS = 32


def padded_2(array, sides, width):
    for axis, dim in sides:
        peers, length = (lax.axis_size(axis), array.shape[dim])
        up = [(i, (i + 1) % peers) for i in range(peers - 1)]
        down = [(j, i) for i, j in up]
        last = lax.slice_in_dim(array, length - width, length, axis=dim)
        leading = lax.slice_in_dim(array, 0, width, axis=dim)
        before = lax.ppermute(last, axis, up)
        after = lax.ppermute(leading, axis, down)
        array = jnp.concatenate([before, array, after], axis=dim)
    return array


def shifted_2(value, axis, steps):
    count = lax.axis_size(axis)
    pairs = [(source, (source + steps) % count) for source in range(count)]
    return lax.ppermute(value, axis, pairs)


def conv_plane(field, weight, bias):
    rows_n, frames_n, cols_n, chans = field.shape
    padded = jnp.pad(field, ((1, 1), (0, 0), (1, 1), (0, 0)))
    total = jnp.zeros((rows_n * frames_n * cols_n, weight.shape[3]), jnp.float32)
    for row_off in range(3):
        for col_off in range(3):
            window = padded[row_off : row_off + rows_n, :, col_off : col_off + cols_n, :].reshape(
                -1, chans
            )
            total = total + jnp.dot(
                window, weight[row_off, col_off], preferred_element_type=jnp.float32
            )
    return total.reshape(rows_n, frames_n, cols_n, -1) + bias


def layer_norm(field, token_gain):
    flat = field.astype(jnp.float32)
    token_mean = jnp.mean(flat, axis=-1, keepdims=True)
    shifted = flat - token_mean
    token_var = jnp.mean(shifted * shifted, axis=-1, keepdims=True)
    return (shifted / jnp.sqrt(token_var + 1e-05) * token_gain).astype(jnp.bfloat16)


def attend(queries, carried, keys, values):
    block = queries.shape[0]
    head_count = queries.shape[1]
    block_count = keys.shape[0] // block
    key_blocks = keys.reshape(block_count, block, head_count, HD)
    value_blocks = values.reshape(block_count, block, head_count, HD)
    scale = 1.0 / math.sqrt(HD)

    def visit_block(state, block_pair):
        running_max, denominator, numerator = state
        key_block, value_block = block_pair
        scores = (
            jnp.einsum("qhd,khd->qhk", queries, key_block, preferred_element_type=jnp.float32)
            * scale
        )
        new_max = jnp.maximum(running_max, jnp.max(scores, axis=-1))
        shrink = jnp.exp(running_max - new_max)
        weights = jnp.exp(scores - new_max[..., None])
        denominator = denominator * shrink + jnp.sum(weights, axis=-1)
        numerator = numerator * shrink[..., None] + jnp.einsum(
            "qhk,khd->qhd",
            weights.astype(jnp.bfloat16),
            value_block,
            preferred_element_type=jnp.float32,
        )
        return ((new_max, denominator, numerator), None)

    result, _ = lax.scan(visit_block, carried, (key_blocks, value_blocks))
    return result


def body(
    latents,
    spatial_weight,
    spatial_bias,
    norm_gain,
    norm_shift,
    temporal_weight,
    temporal_bias,
    token_gain,
    query_weight,
    key_weight,
    value_weight,
    output_weight,
):
    row_count, frame_count, width_cells, channels = latents.shape
    plane = lax.all_gather(latents, "rows", axis=0, tiled=True)
    plane_rows = plane.shape[0]
    local_out = spatial_weight.shape[3]
    spatial = conv_plane(plane, spatial_weight, spatial_bias)
    local_groups = NORM_GROUPS // lax.axis_size("rows")
    grouped = spatial.reshape(plane_rows, frame_count, width_cells, local_groups, -1)
    group_mean = jnp.mean(grouped, axis=(0, 2, 4), keepdims=True)
    centred = grouped - group_mean
    group_var = jnp.mean(centred * centred, axis=(0, 2, 4), keepdims=True)
    scaled = (centred / jnp.sqrt(group_var + 1e-05)).reshape(
        plane_rows, frame_count, width_cells, local_out
    ) * norm_gain + norm_shift
    activated = jax.nn.silu(scaled).astype(jnp.bfloat16)
    rim = padded_2(activated, (("frames", 1),), 1)
    row_total = row_count * lax.axis_size("rows")
    row_piece = rim
    total = jnp.zeros((row_total * frame_count * width_cells, channels), jnp.float32)
    for lag_index in range(3):
        window = row_piece[:, lag_index : lag_index + frame_count].reshape(-1, local_out)
        total = total + jnp.dot(
            window, temporal_weight[lag_index], preferred_element_type=jnp.float32
        )
    temporal = lax.psum_scatter(
        total.reshape(row_total, frame_count, width_cells, channels).astype(jnp.bfloat16),
        "rows",
        scatter_dimension=0,
        tiled=True,
    ).astype(jnp.float32)
    hidden = (latents.astype(jnp.float32) + temporal + temporal_bias).astype(jnp.bfloat16)
    normed_all = lax.all_gather(layer_norm(hidden, token_gain), "rows", axis=0, tiled=True)
    flat = normed_all.reshape(-1, channels)
    head_cols = query_weight.shape[1]
    head_count = head_cols // HD
    token_count = flat.shape[0]
    queries = jnp.dot(flat, query_weight, preferred_element_type=jnp.float32).astype(jnp.bfloat16)
    keys = jnp.dot(flat, key_weight, preferred_element_type=jnp.float32).astype(jnp.bfloat16)
    values = jnp.dot(flat, value_weight, preferred_element_type=jnp.float32).astype(jnp.bfloat16)
    start_state = (
        jnp.full((token_count, head_count), -1e30, jnp.float32),
        jnp.zeros((token_count, head_count), jnp.float32),
        jnp.zeros((token_count, head_count, HD), jnp.float32),
    )
    local_keys = keys.reshape(token_count, head_count, HD)
    local_values = values.reshape(token_count, head_count, HD)

    def travel(turn, state):
        query_moving, running_max, denominator, numerator = state
        running_max, denominator, numerator = attend(
            query_moving, (running_max, denominator, numerator), local_keys, local_values
        )
        return (
            shifted_2(query_moving, "frames", 1),
            shifted_2(running_max.astype(jnp.bfloat16), "frames", 1).astype(running_max.dtype),
            shifted_2(denominator.astype(jnp.bfloat16), "frames", 1).astype(denominator.dtype),
            shifted_2(numerator.astype(jnp.bfloat16), "frames", 1).astype(numerator.dtype),
        )

    start_moving = queries.reshape(token_count, head_count, HD)
    final = lax.fori_loop(0, lax.axis_size("frames"), travel, (start_moving,) + start_state)
    denominator, numerator = (final[2], final[3])
    attended = (
        (numerator / denominator[..., None])
        .astype(jnp.bfloat16)
        .reshape(plane_rows, frame_count, width_cells, head_cols)
    )
    row_piece = attended
    mixed = lax.psum_scatter(
        jnp.dot(row_piece.reshape(-1, head_cols), output_weight, preferred_element_type=jnp.float32)
        .reshape(row_count * lax.axis_size("rows"), frame_count, width_cells, channels)
        .astype(jnp.bfloat16),
        "rows",
        scatter_dimension=0,
        tiled=True,
    ).astype(jnp.float32)
    return (hidden.astype(jnp.float32) + mixed).astype(jnp.bfloat16)


MESH = pl.DeviceIdType.MESH
DMA = pltpu.SemaphoreType.DMA
VMEM_SPEC = pl.BlockSpec(memory_space=pltpu.VMEM)
ANY_SPEC = pl.BlockSpec(memory_space=pl.ANY)
BF16 = jnp.bfloat16
F32 = jnp.float32
VMEM_LIMIT = 54 << 20
PARTS = 2


def remote(src, dst, send, recv, axis, peer):
    return pltpu.make_async_remote_copy(
        src_ref=src,
        dst_ref=dst,
        send_sem=send,
        recv_sem=recv,
        device_id={axis: peer},
        device_id_type=MESH,
    )


def greet(barrier, axis, peer):
    pl.semaphore_signal(barrier, inc=1, device_id={axis: peer}, device_id_type=MESH)


class Gather:
    def __init__(self, block, out, send, recv):
        me = lax.axis_index("rows")
        near, far = me ^ 1, me ^ 2
        step = block.shape[0] // PARTS
        self.far, self.onward = [], []
        for part in range(PARTS):
            piece = pl.ds(part * step, step)
            self.far.append(
                remote(
                    block.at[piece],
                    out.at[me, piece],
                    send.at[part],
                    recv.at[part],
                    "rows",
                    far,
                )
            )
            self.onward.append(
                remote(
                    out.at[far, piece],
                    out.at[far, piece],
                    send.at[PARTS + part],
                    recv.at[PARTS + part],
                    "rows",
                    near,
                )
            )
        self.near = remote(
            block, out.at[me], send.at[2 * PARTS], recv.at[2 * PARTS], "rows", near
        )

    def start(self):
        for copy in self.far:
            copy.start()
        self.near.start()

    def near_ready(self):
        self.near.wait_recv()

    def finish(self):
        for copy, onward in zip(self.far, self.onward):
            copy.wait_recv()
            onward.start()
        for copy in self.far:
            copy.wait_send()
        self.near.wait_send()
        for onward in self.onward:
            onward.wait()


def reduce_rows(term, sent, got_near, got_far, send, recv):
    me = lax.axis_index("rows")
    near, far = me ^ 1, me ^ 2

    def hand(slot, value):
        sent[slot] = value.astype(BF16)
        copy = remote(
            sent.at[slot], got_near.at[slot], send.at[slot], recv.at[slot], "rows", near
        )
        copy.start()
        return copy

    first = hand(0, term(far ^ 1, 0))
    mine = term(far, 1)
    first.wait_recv()
    sent[2] = (mine + got_near[0].astype(F32)).astype(BF16)
    across = remote(sent.at[2], got_far, send.at[2], recv.at[2], "rows", far)
    across.start()
    second = hand(1, term(near, 2))
    mine = term(me, 3)
    second.wait_recv()
    mine = mine + got_near[1].astype(F32)
    across.wait_recv()
    total = mine + got_far[...].astype(F32)
    for copy in (first, second, across):
        copy.wait_send()
    return total


def row(ref):
    return ref[...].reshape(1, -1)


def convolve(plane, shifted, weight, width):
    blocks, size, channels = plane.shape
    tokens = blocks * size
    edge = jnp.zeros((width, channels), BF16)
    column = lax.broadcasted_iota(jnp.int32, (size, channels), 0) % width
    for offset in range(3):
        shifted[offset, :width, :] = edge
        shifted[offset, tokens + width :, :] = edge
    for block in range(blocks):
        rows = slice(width + block * size, width + (block + 1) * size)
        value = plane[block]
        wide = value.astype(F32)
        before = jnp.where(column == 0, 0.0, pltpu.roll(wide, 1, 0))
        after = jnp.where(column == width - 1, 0.0, pltpu.roll(wide, size - 1, 0))
        shifted[0, rows, :] = before.astype(BF16)
        shifted[1, rows, :] = value
        shifted[2, rows, :] = after.astype(BF16)
    total = None
    for row_off in range(3):
        for col_off in range(3):
            window = shifted[col_off, row_off * width : row_off * width + tokens, :]
            part = lax.dot_general(
                window,
                weight[row_off, col_off],
                (((1,), (1,)), ((), ())),
                preferred_element_type=F32,
            )
            total = part if total is None else total + part
    return total


def group_norm_silu(spatial, gain, shift, groups):
    tokens, channels = spatial.shape
    per = channels // groups
    lane = lax.broadcasted_iota(jnp.int32, (groups, channels), 1)
    first = lax.broadcasted_iota(jnp.int32, (groups, channels), 0) * per
    member = jnp.logical_and(lane >= first, lane < first + per)

    def group_mean(value):
        column = jnp.sum(value, axis=0, keepdims=True)
        sums = jnp.sum(jnp.where(member, column, 0.0), axis=1, keepdims=True)
        return jnp.sum(jnp.where(member, sums, 0.0), axis=0, keepdims=True) / (tokens * per)

    centred = spatial - group_mean(spatial)
    scale = 1.0 / jnp.sqrt(group_mean(centred * centred) + 1e-05)
    value = centred * scale * gain + shift
    return (value / (1.0 + jnp.exp(-value))).astype(BF16)


def block_kernel(
    frames,
    width_cells,
    groups,
    latents_hbm,
    spatial_hbm,
    spatial_bias,
    norm_gain,
    norm_shift,
    temporal_hbm,
    temporal_bias,
    token_gain,
    query_hbm,
    key_hbm,
    value_hbm,
    output_hbm,
    out_ref,
    latents,
    spatial_w,
    temporal_w,
    project_w,
    output_w,
    plane,
    shifted,
    act,
    halo,
    normed,
    normed_all,
    outgoing,
    got,
    keys,
    values,
    probs,
    done,
    back,
    att,
    sent,
    got_near,
    got_far,
    load_sem,
    lat_send,
    lat_recv,
    halo_send,
    halo_recv,
    gat_send,
    gat_recv,
    in_send,
    in_recv,
    out_send,
    out_recv,
    sum_send,
    sum_recv,
):
    me = lax.axis_index("rows")
    frame = lax.axis_index("frames")
    near, far = me ^ 1, me ^ 2
    loads = []
    for index, (src, dst) in enumerate(
        (
            (latents_hbm, latents),
            (spatial_hbm, spatial_w),
            (temporal_hbm, temporal_w),
            (key_hbm, project_w.at[0]),
            (query_hbm, project_w.at[1]),
            (value_hbm, project_w.at[2]),
            (output_hbm, output_w),
        )
    ):
        load = pltpu.make_async_copy(src, dst, load_sem.at[index])
        load.start()
        loads.append(load)
    barrier = pltpu.get_barrier_semaphore()
    greet(barrier, "rows", near)
    greet(barrier, "rows", far)
    for turn in range(1, frames):
        greet(barrier, "frames", lax.rem(frame + turn, frames))
    pl.semaphore_wait(barrier, frames + 1)

    loads[0].wait()
    gather = Gather(latents, plane, lat_send, lat_recv)
    gather.start()
    plane[me] = latents[...]
    gather.near_ready()
    gather.finish()
    loads[1].wait()
    spatial = convolve(plane, shifted, spatial_w, width_cells) + row(spatial_bias)
    act[...] = group_norm_silu(spatial, row(norm_gain), row(norm_shift), groups)

    has_prev, has_next = frame > 0, frame < frames - 1
    prev = jnp.maximum(frame - 1, 0)
    later = jnp.minimum(frame + 1, frames - 1)
    size = latents.shape[0]

    def rows_of(block):
        return pl.ds(pl.multiple_of(block * size, size), size)

    up, down = [], []
    for turn, block in enumerate((far ^ 1, far, near, me)):
        rows = rows_of(block)
        for side, (copies, peer) in enumerate(((up, later), (down, prev))):
            copies.append(
                remote(
                    act.at[rows],
                    halo.at[side, rows],
                    halo_send.at[side, turn],
                    halo_recv.at[side, turn],
                    "frames",
                    peer,
                )
            )

    @pl.when(has_next)
    def _():
        for copy in up:
            copy.start()

    @pl.when(has_prev)
    def _():
        for copy in down:
            copy.start()

    @pl.when(jnp.logical_not(has_prev))
    def _():
        halo[0] = jnp.zeros(halo.shape[1:], halo.dtype)

    @pl.when(jnp.logical_not(has_next))
    def _():
        halo[1] = jnp.zeros(halo.shape[1:], halo.dtype)

    loads[2].wait()

    def temporal_term(block, turn):
        rows = rows_of(block)
        total = jnp.dot(act[rows, :], temporal_w[1], preferred_element_type=F32)

        @pl.when(has_prev)
        def _():
            up[turn].wait_recv()

        @pl.when(has_next)
        def _():
            down[turn].wait_recv()

        total += jnp.dot(halo[0, rows, :], temporal_w[0], preferred_element_type=F32)
        total += jnp.dot(halo[1, rows, :], temporal_w[2], preferred_element_type=F32)
        return total

    temporal = reduce_rows(
        temporal_term, sent.at[0], got_near.at[0], got_far.at[0], sum_send.at[0], sum_recv.at[0]
    )

    @pl.when(has_next)
    def _():
        for copy in up:
            copy.wait_send()

    @pl.when(has_prev)
    def _():
        for copy in down:
            copy.wait_send()

    hidden = (latents[...].astype(F32) + temporal + row(temporal_bias)).astype(BF16)
    flat = hidden.astype(F32)
    centred = flat - jnp.mean(flat, axis=-1, keepdims=True)
    var = jnp.mean(centred * centred, axis=-1, keepdims=True)
    normed[...] = (centred / jnp.sqrt(var + 1e-05) * row(token_gain)).astype(BF16)
    gather = Gather(normed, normed_all, gat_send, gat_recv)
    gather.start()
    normed_all[me] = normed[...]

    tokens = act.shape[0]
    width, half = got.shape[3], got.shape[4]
    here = me // 2
    moves = [[], [], []]

    def project(pair):
        slab = normed_all[pl.ds(2 * pair, 2)].reshape(half, -1)
        for kind in range(3):
            cols = jnp.dot(slab, project_w[kind], preferred_element_type=F32)
            cols = cols.T.astype(BF16)
            for owner in range(frames):
                outgoing[kind, pair, owner] = cols[owner * width : (owner + 1) * width, :]
            for turn in range(1, frames):
                peer = lax.rem(frame + turn, frames)
                copy = remote(
                    outgoing.at[kind, pair, peer],
                    got.at[kind, pair, frame],
                    in_send.at[kind, pair, turn],
                    in_recv.at[kind, pair, turn],
                    "frames",
                    peer,
                )
                copy.start()
                moves[kind].append(copy)
            got[kind, pair, frame] = outgoing[kind, pair, frame]

    for kind in range(3):
        loads[3 + kind].wait()
    gather.near_ready()
    project(here)
    gather.finish()
    project(1 - here)

    for copy in moves[0]:
        copy.wait_recv()
    for source in range(frames):
        for pair in range(2):
            begin = source * tokens + pair * half
            keys[begin : begin + half, :] = got[0, pair, source].astype(F32).T.astype(BF16)
    for copy in moves[1]:
        copy.wait_recv()
    scale = 1.0 / math.sqrt(HD)
    heads = width // HD
    sums = []
    for turn in range(1, frames + 1):
        peer = lax.rem(frame + turn, frames)
        for head in range(heads):
            cols = slice(head * HD, (head + 1) * HD)
            query = jnp.concatenate(
                [got[1, 0, peer, cols, :], got[1, 1, peer, cols, :]], axis=1
            )
            scores = jnp.dot(keys[:, cols], query, preferred_element_type=F32) * scale
            weights = jnp.exp(scores - jnp.max(scores, axis=0, keepdims=True))
            sums.append(jnp.sum(weights, axis=0, keepdims=True))
            probs[(turn - 1) * heads + head] = weights.astype(BF16)
    for copy in moves[2]:
        copy.wait_recv()
    for source in range(frames):
        for pair in range(2):
            begin = source * tokens + pair * half
            values[:, begin : begin + half] = got[2, pair, source]
    returns = [[], []]

    def give_back(step, pair, turn):
        peer = lax.rem(frame + turn, frames)
        copy = remote(
            done.at[pair, peer],
            back.at[pair, frame],
            out_send.at[pair, turn],
            out_recv.at[pair, turn],
            "frames",
            peer,
        )
        copy.start()
        returns[step].append(copy)

    for turn in range(1, frames + 1):
        peer = lax.rem(frame + turn, frames)
        for head in range(heads):
            cols = slice(head * HD, (head + 1) * HD)
            place = (turn - 1) * heads + head
            numerator = jnp.dot(values[cols, :], probs[place], preferred_element_type=F32)
            result = (numerator / sums[place]).astype(BF16)
            for pair in range(2):
                done[pair, peer, cols, :] = result[:, pair * half : (pair + 1) * half]
        if turn < frames:
            give_back(0, 1 - here, turn)
    for turn in range(1, frames):
        give_back(1, here, turn)
    for pair in range(2):
        back[pair, frame] = done[pair, frame]
    loads[6].wait()

    def collect(step, pair):
        for copy in returns[step]:
            copy.wait_recv()
        rows = pl.ds(pl.multiple_of(pair * half, half), half)
        for source in range(frames):
            att[rows, source * width : (source + 1) * width] = (
                back[pair, source].astype(F32).T.astype(BF16)
            )

    def mixed_term(block, turn):
        if turn == 0:
            collect(0, 1 - here)
        if turn == 2:
            collect(1, here)
        return jnp.dot(att[rows_of(block), :], output_w[...], preferred_element_type=F32)

    mixed = reduce_rows(
        mixed_term, sent.at[1], got_near.at[1], got_far.at[1], sum_send.at[1], sum_recv.at[1]
    )
    out_ref[...] = (hidden.astype(F32) + mixed).astype(BF16)
    for batch in moves + returns:
        for copy in batch:
            copy.wait_send()


def body_fast(
    latents,
    spatial_weight,
    spatial_bias,
    norm_gain,
    norm_shift,
    temporal_weight,
    temporal_bias,
    token_gain,
    query_weight,
    key_weight,
    value_weight,
    output_weight,
):
    channels = latents.shape[3]
    peers, frames = lax.axis_size("rows"), lax.axis_size("frames")
    block = latents.reshape(-1, channels)
    size = block.shape[0]
    tokens = size * peers
    width_cells = latents.shape[2]
    local_out = spatial_weight.shape[3]
    width = query_weight.shape[1] // frames
    heads = width // HD
    links = 2 * PARTS + 1
    denoised = pl.pallas_call(
        functools.partial(block_kernel, frames, width_cells, NORM_GROUPS // peers),
        out_shape=jax.ShapeDtypeStruct(block.shape, BF16),
        in_specs=[ANY_SPEC] * 2
        + [VMEM_SPEC] * 3
        + [ANY_SPEC]
        + [VMEM_SPEC] * 2
        + [ANY_SPEC] * 4,
        out_specs=VMEM_SPEC,
        scratch_shapes=[
            pltpu.VMEM(block.shape, BF16),
            pltpu.VMEM(spatial_weight.shape[:2] + (local_out, channels), BF16),
            pltpu.VMEM(temporal_weight.shape, BF16),
            pltpu.VMEM((3,) + query_weight.shape, BF16),
            pltpu.VMEM(output_weight.shape, BF16),
            pltpu.VMEM((peers,) + block.shape, BF16),
            pltpu.VMEM((3, tokens + 2 * width_cells, channels), BF16),
            pltpu.VMEM((tokens, local_out), BF16),
            pltpu.VMEM((2, tokens, local_out), BF16),
            pltpu.VMEM(block.shape, BF16),
            pltpu.VMEM((peers,) + block.shape, BF16),
            pltpu.VMEM((3, 2, frames, width, tokens // 2), BF16),
            pltpu.VMEM((3, 2, frames, width, tokens // 2), BF16),
            pltpu.VMEM((frames * tokens, width), BF16),
            pltpu.VMEM((width, frames * tokens), BF16),
            pltpu.VMEM((frames * heads, frames * tokens, tokens), BF16),
            pltpu.VMEM((2, frames, width, tokens // 2), BF16),
            pltpu.VMEM((2, frames, width, tokens // 2), BF16),
            pltpu.VMEM((tokens, frames * width), BF16),
            pltpu.VMEM((2, 3) + block.shape, BF16),
            pltpu.VMEM((2, 2) + block.shape, BF16),
            pltpu.VMEM((2,) + block.shape, BF16),
            DMA((7,)),
            DMA((links,)),
            DMA((links,)),
            DMA((2, peers)),
            DMA((2, peers)),
            DMA((links,)),
            DMA((links,)),
            DMA((3, 2, frames)),
            DMA((3, 2, frames)),
            DMA((2, frames)),
            DMA((2, frames)),
            DMA((2, 3)),
            DMA((2, 3)),
        ],
        compiler_params=pltpu.CompilerParams(
            collective_id=0, has_side_effects=True, vmem_limit_bytes=VMEM_LIMIT
        ),
    )(
        block,
        jnp.swapaxes(spatial_weight, 2, 3),
        spatial_bias,
        norm_gain,
        norm_shift,
        temporal_weight,
        temporal_bias,
        token_gain,
        query_weight,
        key_weight,
        value_weight,
        output_weight,
    )
    return denoised.reshape(latents.shape)


def fits(mesh):
    def choose(*args):
        latents, query_weight = args[0], args[8]
        peers, frames = mesh.shape["rows"], mesh.shape["frames"]
        heads = query_weight.shape[1] // HD
        tokens = latents.shape[0] * latents.shape[1] * latents.shape[2] * peers
        fast = (
            peers == 4
            and latents.shape[1] == 1
            and heads % frames == 0
            and tokens % 256 == 0
            and latents.shape[2] % 16 == 0
            and latents.shape[0] * latents.shape[2] % (16 * PARTS) == 0
        )
        return (body_fast if fast else body)(*args)

    return choose


def solution(mesh):
    in_specs = (
        P("rows", ("groups", "frames"), None, None),
        P(None, None, None, "rows"),
        P("rows"),
        P("rows"),
        P("rows"),
        P(None, "rows", None),
        P(),
        P(),
        P(None, "rows"),
        P(None, "rows"),
        P(None, "rows"),
        P("rows", None),
    )
    out_specs = P("rows", ("groups", "frames"), None, None)
    return jax.shard_map(
        fits(mesh), mesh=mesh, in_specs=in_specs, out_specs=out_specs, check_vma=False
    )
```

```python
import functools
import math

import jax
import jax.numpy as jnp
from jax import lax
from jax.experimental import pallas as pl
from jax.experimental.pallas import tpu as pltpu
from jax.sharding import PartitionSpec as P

HD = 64
NORM_GROUPS = 32


def padded_2(array, sides, width):
    for axis, dim in sides:
        peers, length = (lax.axis_size(axis), array.shape[dim])
        up = [(i, (i + 1) % peers) for i in range(peers - 1)]
        down = [(j, i) for i, j in up]
        last = lax.slice_in_dim(array, length - width, length, axis=dim)
        leading = lax.slice_in_dim(array, 0, width, axis=dim)
        before = lax.ppermute(last, axis, up)
        after = lax.ppermute(leading, axis, down)
        array = jnp.concatenate([before, array, after], axis=dim)
    return array


def shifted_2(value, axis, steps):
    count = lax.axis_size(axis)
    pairs = [(source, (source + steps) % count) for source in range(count)]
    return lax.ppermute(value, axis, pairs)


def conv_plane(field, weight, bias):
    rows_n, frames_n, cols_n, chans = field.shape
    padded = jnp.pad(field, ((1, 1), (0, 0), (1, 1), (0, 0)))
    total = jnp.zeros((rows_n * frames_n * cols_n, weight.shape[3]), jnp.float32)
    for row_off in range(3):
        for col_off in range(3):
            window = padded[row_off : row_off + rows_n, :, col_off : col_off + cols_n, :].reshape(
                -1, chans
            )
            total = total + jnp.dot(
                window, weight[row_off, col_off], preferred_element_type=jnp.float32
            )
    return total.reshape(rows_n, frames_n, cols_n, -1) + bias


def layer_norm(field, token_gain):
    flat = field.astype(jnp.float32)
    token_mean = jnp.mean(flat, axis=-1, keepdims=True)
    shifted = flat - token_mean
    token_var = jnp.mean(shifted * shifted, axis=-1, keepdims=True)
    return (shifted / jnp.sqrt(token_var + 1e-05) * token_gain).astype(jnp.bfloat16)


def attend(queries, carried, keys, values):
    block = queries.shape[0]
    head_count = queries.shape[1]
    block_count = keys.shape[0] // block
    key_blocks = keys.reshape(block_count, block, head_count, HD)
    value_blocks = values.reshape(block_count, block, head_count, HD)
    scale = 1.0 / math.sqrt(HD)

    def visit_block(state, block_pair):
        running_max, denominator, numerator = state
        key_block, value_block = block_pair
        scores = (
            jnp.einsum("qhd,khd->qhk", queries, key_block, preferred_element_type=jnp.float32)
            * scale
        )
        new_max = jnp.maximum(running_max, jnp.max(scores, axis=-1))
        shrink = jnp.exp(running_max - new_max)
        weights = jnp.exp(scores - new_max[..., None])
        denominator = denominator * shrink + jnp.sum(weights, axis=-1)
        numerator = numerator * shrink[..., None] + jnp.einsum(
            "qhk,khd->qhd",
            weights.astype(jnp.bfloat16),
            value_block,
            preferred_element_type=jnp.float32,
        )
        return ((new_max, denominator, numerator), None)

    result, _ = lax.scan(visit_block, carried, (key_blocks, value_blocks))
    return result


def body(
    latents,
    spatial_weight,
    spatial_bias,
    norm_gain,
    norm_shift,
    temporal_weight,
    temporal_bias,
    token_gain,
    query_weight,
    key_weight,
    value_weight,
    output_weight,
):
    row_count, frame_count, width_cells, channels = latents.shape
    plane = lax.all_gather(latents, "rows", axis=0, tiled=True)
    plane_rows = plane.shape[0]
    local_out = spatial_weight.shape[3]
    spatial = conv_plane(plane, spatial_weight, spatial_bias)
    local_groups = NORM_GROUPS // lax.axis_size("rows")
    grouped = spatial.reshape(plane_rows, frame_count, width_cells, local_groups, -1)
    group_mean = jnp.mean(grouped, axis=(0, 2, 4), keepdims=True)
    centred = grouped - group_mean
    group_var = jnp.mean(centred * centred, axis=(0, 2, 4), keepdims=True)
    scaled = (centred / jnp.sqrt(group_var + 1e-05)).reshape(
        plane_rows, frame_count, width_cells, local_out
    ) * norm_gain + norm_shift
    activated = jax.nn.silu(scaled).astype(jnp.bfloat16)
    rim = padded_2(activated, (("frames", 1),), 1)
    row_total = row_count * lax.axis_size("rows")
    row_piece = rim
    total = jnp.zeros((row_total * frame_count * width_cells, channels), jnp.float32)
    for lag_index in range(3):
        window = row_piece[:, lag_index : lag_index + frame_count].reshape(-1, local_out)
        total = total + jnp.dot(
            window, temporal_weight[lag_index], preferred_element_type=jnp.float32
        )
    temporal = lax.psum_scatter(
        total.reshape(row_total, frame_count, width_cells, channels).astype(jnp.bfloat16),
        "rows",
        scatter_dimension=0,
        tiled=True,
    ).astype(jnp.float32)
    hidden = (latents.astype(jnp.float32) + temporal + temporal_bias).astype(jnp.bfloat16)
    normed_all = lax.all_gather(layer_norm(hidden, token_gain), "rows", axis=0, tiled=True)
    flat = normed_all.reshape(-1, channels)
    head_cols = query_weight.shape[1]
    head_count = head_cols // HD
    token_count = flat.shape[0]
    queries = jnp.dot(flat, query_weight, preferred_element_type=jnp.float32).astype(jnp.bfloat16)
    keys = jnp.dot(flat, key_weight, preferred_element_type=jnp.float32).astype(jnp.bfloat16)
    values = jnp.dot(flat, value_weight, preferred_element_type=jnp.float32).astype(jnp.bfloat16)
    start_state = (
        jnp.full((token_count, head_count), -1e30, jnp.float32),
        jnp.zeros((token_count, head_count), jnp.float32),
        jnp.zeros((token_count, head_count, HD), jnp.float32),
    )
    local_keys = keys.reshape(token_count, head_count, HD)
    local_values = values.reshape(token_count, head_count, HD)

    def travel(turn, state):
        query_moving, running_max, denominator, numerator = state
        running_max, denominator, numerator = attend(
            query_moving, (running_max, denominator, numerator), local_keys, local_values
        )
        return (
            shifted_2(query_moving, "frames", 1),
            shifted_2(running_max.astype(jnp.bfloat16), "frames", 1).astype(running_max.dtype),
            shifted_2(denominator.astype(jnp.bfloat16), "frames", 1).astype(denominator.dtype),
            shifted_2(numerator.astype(jnp.bfloat16), "frames", 1).astype(numerator.dtype),
        )

    start_moving = queries.reshape(token_count, head_count, HD)
    final = lax.fori_loop(0, lax.axis_size("frames"), travel, (start_moving,) + start_state)
    denominator, numerator = (final[2], final[3])
    attended = (
        (numerator / denominator[..., None])
        .astype(jnp.bfloat16)
        .reshape(plane_rows, frame_count, width_cells, head_cols)
    )
    row_piece = attended
    mixed = lax.psum_scatter(
        jnp.dot(row_piece.reshape(-1, head_cols), output_weight, preferred_element_type=jnp.float32)
        .reshape(row_count * lax.axis_size("rows"), frame_count, width_cells, channels)
        .astype(jnp.bfloat16),
        "rows",
        scatter_dimension=0,
        tiled=True,
    ).astype(jnp.float32)
    return (hidden.astype(jnp.float32) + mixed).astype(jnp.bfloat16)


MESH = pl.DeviceIdType.MESH
DMA = pltpu.SemaphoreType.DMA
VMEM_SPEC = pl.BlockSpec(memory_space=pltpu.VMEM)
ANY_SPEC = pl.BlockSpec(memory_space=pl.ANY)
BF16 = jnp.bfloat16
F32 = jnp.float32
VMEM_LIMIT = 54 << 20
PARTS = 2


def remote(src, dst, send, recv, axis, peer):
    return pltpu.make_async_remote_copy(
        src_ref=src,
        dst_ref=dst,
        send_sem=send,
        recv_sem=recv,
        device_id={axis: peer},
        device_id_type=MESH,
    )


def greet(barrier, axis, peer):
    pl.semaphore_signal(barrier, inc=1, device_id={axis: peer}, device_id_type=MESH)


class Gather:
    def __init__(self, block, out, send, recv):
        me = lax.axis_index("rows")
        near, far = me ^ 1, me ^ 2
        step = block.shape[0] // PARTS
        self.far, self.onward = [], []
        for part in range(PARTS):
            piece = pl.ds(part * step, step)
            self.far.append(
                remote(
                    block.at[piece],
                    out.at[me, piece],
                    send.at[part],
                    recv.at[part],
                    "rows",
                    far,
                )
            )
            self.onward.append(
                remote(
                    out.at[far, piece],
                    out.at[far, piece],
                    send.at[PARTS + part],
                    recv.at[PARTS + part],
                    "rows",
                    near,
                )
            )
        self.near = remote(
            block, out.at[me], send.at[2 * PARTS], recv.at[2 * PARTS], "rows", near
        )

    def start(self):
        for copy in self.far:
            copy.start()
        self.near.start()

    def near_ready(self):
        self.near.wait_recv()

    def finish(self):
        for copy, onward in zip(self.far, self.onward):
            copy.wait_recv()
            onward.start()
        for copy in self.far:
            copy.wait_send()
        self.near.wait_send()
        for onward in self.onward:
            onward.wait()


def reduce_rows(term, sent, got_near, got_far, send, recv):
    me = lax.axis_index("rows")
    near, far = me ^ 1, me ^ 2

    def hand(slot, value):
        sent[slot] = value.astype(BF16)
        copy = remote(
            sent.at[slot], got_near.at[slot], send.at[slot], recv.at[slot], "rows", near
        )
        copy.start()
        return copy

    first = hand(0, term(far ^ 1, 0))
    mine = term(far, 1)
    first.wait_recv()
    sent[2] = (mine + got_near[0].astype(F32)).astype(BF16)
    across = remote(sent.at[2], got_far, send.at[2], recv.at[2], "rows", far)
    across.start()
    second = hand(1, term(near, 2))
    mine = term(me, 3)
    second.wait_recv()
    mine = mine + got_near[1].astype(F32)
    across.wait_recv()
    total = mine + got_far[...].astype(F32)
    for copy in (first, second, across):
        copy.wait_send()
    return total


def row(ref):
    return ref[...].reshape(1, -1)


def clear_edges(shifted, width, row_after):
    edge = jnp.zeros((width, shifted.shape[2]), BF16)
    tall = shifted.shape[1]
    for offset in range(3):
        shifted[offset, :width, :] = edge
        shifted[offset, tall - width :, :] = edge
        shifted[offset, pl.ds(pl.multiple_of(row_after, width), width), :] = edge


def shift_block(value, shifted, block, width):
    size = value.shape[0]
    column = lax.broadcasted_iota(jnp.int32, value.shape, 0) % width
    rows = pl.ds(pl.multiple_of(width + block * size, width), size)
    wide = value.astype(F32)
    before = jnp.where(column == 0, 0.0, pltpu.roll(wide, 1, 0))
    after = jnp.where(column == width - 1, 0.0, pltpu.roll(wide, size - 1, 0))
    shifted[0, rows, :] = before.astype(BF16)
    shifted[1, rows, :] = value
    shifted[2, rows, :] = after.astype(BF16)


def tap(shifted, weight, begin, count, width, row_off, col_off):
    return lax.dot_general(
        shifted[col_off, pl.ds(pl.multiple_of(begin, width), count), :],
        weight[row_off, col_off],
        (((1,), (1,)), ((), ())),
        preferred_element_type=F32,
    )


def convolve(shifted, weight, begin, count, width):
    total = None
    for row_off in range(3):
        for col_off in range(3):
            part = tap(
                shifted, weight, begin + row_off * width, count, width, row_off, col_off
            )
            total = part if total is None else total + part
    return total


def group_norm_silu(spatial, gain, shift, groups):
    tokens, channels = spatial.shape
    per = channels // groups
    lane = lax.broadcasted_iota(jnp.int32, (groups, channels), 1)
    first = lax.broadcasted_iota(jnp.int32, (groups, channels), 0) * per
    member = jnp.logical_and(lane >= first, lane < first + per)

    def group_mean(value):
        column = jnp.sum(value, axis=0, keepdims=True)
        sums = jnp.sum(jnp.where(member, column, 0.0), axis=1, keepdims=True)
        return jnp.sum(jnp.where(member, sums, 0.0), axis=0, keepdims=True) / (tokens * per)

    centred = spatial - group_mean(spatial)
    scale = 1.0 / jnp.sqrt(group_mean(centred * centred) + 1e-05)
    value = centred * scale * gain + shift
    return (value / (1.0 + jnp.exp(-value))).astype(BF16)


def block_kernel(
    frames,
    width_cells,
    groups,
    latents_hbm,
    spatial_hbm,
    spatial_bias,
    norm_gain,
    norm_shift,
    temporal_hbm,
    temporal_bias,
    token_gain,
    query_hbm,
    key_hbm,
    value_hbm,
    output_hbm,
    out_ref,
    latents,
    spatial_w,
    temporal_w,
    project_w,
    output_w,
    plane,
    shifted,
    conv,
    act,
    halo,
    normed,
    normed_all,
    outgoing,
    got,
    keys,
    values,
    probs,
    done,
    back,
    att,
    sent,
    got_near,
    got_far,
    load_sem,
    lat_send,
    lat_recv,
    halo_send,
    halo_recv,
    gat_send,
    gat_recv,
    in_send,
    in_recv,
    out_send,
    out_recv,
    sum_send,
    sum_recv,
):
    me = lax.axis_index("rows")
    frame = lax.axis_index("frames")
    near, far = me ^ 1, me ^ 2
    loads = []
    for index, (src, dst) in enumerate(
        (
            (latents_hbm, latents),
            (spatial_hbm, spatial_w),
            (temporal_hbm, temporal_w),
            (key_hbm, project_w.at[0]),
            (query_hbm, project_w.at[1]),
            (value_hbm, project_w.at[2]),
            (output_hbm, output_w),
        )
    ):
        load = pltpu.make_async_copy(src, dst, load_sem.at[index])
        load.start()
        loads.append(load)
    barrier = pltpu.get_barrier_semaphore()
    greet(barrier, "rows", near)
    greet(barrier, "rows", far)
    for turn in range(1, frames):
        greet(barrier, "frames", lax.rem(frame + turn, frames))
    pl.semaphore_wait(barrier, frames + 1)

    loads[0].wait()
    gather = Gather(latents, plane, lat_send, lat_recv)
    gather.start()
    size = latents.shape[0]
    slab = 2 * size
    chip = me // 2
    mine, other = chip * slab, (1 - chip) * slab
    border = slab - width_cells + chip * width_cells
    beyond = slab - chip * width_cells
    clear_edges(shifted, width_cells, beyond + width_cells)
    shift_block(latents[...], shifted, me, width_cells)
    gather.near_ready()
    shift_block(plane[near], shifted, near, width_cells)
    loads[1].wait()
    conv[pl.ds(pl.multiple_of(mine, slab), slab), :] = convolve(
        shifted, spatial_w, mine, slab, width_cells
    )
    gather.finish()
    shift_block(plane[far], shifted, far, width_cells)
    shift_block(plane[far ^ 1], shifted, far ^ 1, width_cells)
    conv[pl.ds(pl.multiple_of(other, slab), slab), :] = convolve(
        shifted, spatial_w, other, slab, width_cells
    )
    line = pl.ds(pl.multiple_of(border, width_cells), width_cells)
    late = conv[line, :]
    for col_off in range(3):
        late += tap(
            shifted,
            spatial_w,
            beyond + width_cells,
            width_cells,
            width_cells,
            2 - 2 * chip,
            col_off,
        )
    conv[line, :] = late
    spatial = conv[...] + row(spatial_bias)
    act[...] = group_norm_silu(spatial, row(norm_gain), row(norm_shift), groups)

    has_prev, has_next = frame > 0, frame < frames - 1
    prev = jnp.maximum(frame - 1, 0)
    later = jnp.minimum(frame + 1, frames - 1)

    def rows_of(block):
        return pl.ds(pl.multiple_of(block * size, size), size)

    up, down = [], []
    for turn, block in enumerate((far ^ 1, far, near, me)):
        rows = rows_of(block)
        for side, (copies, peer) in enumerate(((up, later), (down, prev))):
            copies.append(
                remote(
                    act.at[rows],
                    halo.at[side, rows],
                    halo_send.at[side, turn],
                    halo_recv.at[side, turn],
                    "frames",
                    peer,
                )
            )

    @pl.when(has_next)
    def _():
        for copy in up:
            copy.start()

    @pl.when(has_prev)
    def _():
        for copy in down:
            copy.start()

    @pl.when(jnp.logical_not(has_prev))
    def _():
        halo[0] = jnp.zeros(halo.shape[1:], halo.dtype)

    @pl.when(jnp.logical_not(has_next))
    def _():
        halo[1] = jnp.zeros(halo.shape[1:], halo.dtype)

    loads[2].wait()

    def temporal_term(block, turn):
        rows = rows_of(block)
        total = jnp.dot(act[rows, :], temporal_w[1], preferred_element_type=F32)

        @pl.when(has_prev)
        def _():
            up[turn].wait_recv()

        @pl.when(has_next)
        def _():
            down[turn].wait_recv()

        total += jnp.dot(halo[0, rows, :], temporal_w[0], preferred_element_type=F32)
        total += jnp.dot(halo[1, rows, :], temporal_w[2], preferred_element_type=F32)
        return total

    temporal = reduce_rows(
        temporal_term, sent.at[0], got_near.at[0], got_far.at[0], sum_send.at[0], sum_recv.at[0]
    )

    @pl.when(has_next)
    def _():
        for copy in up:
            copy.wait_send()

    @pl.when(has_prev)
    def _():
        for copy in down:
            copy.wait_send()

    hidden = (latents[...].astype(F32) + temporal + row(temporal_bias)).astype(BF16)
    flat = hidden.astype(F32)
    centred = flat - jnp.mean(flat, axis=-1, keepdims=True)
    var = jnp.mean(centred * centred, axis=-1, keepdims=True)
    normed[...] = (centred / jnp.sqrt(var + 1e-05) * row(token_gain)).astype(BF16)
    gather = Gather(normed, normed_all, gat_send, gat_recv)
    gather.start()
    normed_all[me] = normed[...]

    tokens = act.shape[0]
    width, half = got.shape[3], got.shape[4]
    here = me // 2
    moves = [[], [], []]

    def project(pair):
        slab = normed_all[pl.ds(2 * pair, 2)].reshape(half, -1)
        for kind in range(3):
            cols = jnp.dot(slab, project_w[kind], preferred_element_type=F32)
            cols = cols.T.astype(BF16)
            for owner in range(frames):
                outgoing[kind, pair, owner] = cols[owner * width : (owner + 1) * width, :]
            for turn in range(1, frames):
                peer = lax.rem(frame + turn, frames)
                copy = remote(
                    outgoing.at[kind, pair, peer],
                    got.at[kind, pair, frame],
                    in_send.at[kind, pair, turn],
                    in_recv.at[kind, pair, turn],
                    "frames",
                    peer,
                )
                copy.start()
                moves[kind].append(copy)
            got[kind, pair, frame] = outgoing[kind, pair, frame]

    for kind in range(3):
        loads[3 + kind].wait()
    gather.near_ready()
    project(here)
    gather.finish()
    project(1 - here)

    for copy in moves[0]:
        copy.wait_recv()
    for source in range(frames):
        for pair in range(2):
            begin = source * tokens + pair * half
            keys[begin : begin + half, :] = got[0, pair, source].astype(F32).T.astype(BF16)
    for copy in moves[1]:
        copy.wait_recv()
    scale = 1.0 / math.sqrt(HD)
    heads = width // HD
    sums = []
    for turn in range(1, frames + 1):
        peer = lax.rem(frame + turn, frames)
        for head in range(heads):
            cols = slice(head * HD, (head + 1) * HD)
            query = jnp.concatenate(
                [got[1, 0, peer, cols, :], got[1, 1, peer, cols, :]], axis=1
            )
            scores = jnp.dot(keys[:, cols], query, preferred_element_type=F32) * scale
            weights = jnp.exp(scores - jnp.max(scores, axis=0, keepdims=True))
            sums.append(jnp.sum(weights, axis=0, keepdims=True))
            probs[(turn - 1) * heads + head] = weights.astype(BF16)
    for copy in moves[2]:
        copy.wait_recv()
    for source in range(frames):
        for pair in range(2):
            begin = source * tokens + pair * half
            values[:, begin : begin + half] = got[2, pair, source]
    returns = [[], []]

    def give_back(step, pair, turn):
        peer = lax.rem(frame + turn, frames)
        copy = remote(
            done.at[pair, peer],
            back.at[pair, frame],
            out_send.at[pair, turn],
            out_recv.at[pair, turn],
            "frames",
            peer,
        )
        copy.start()
        returns[step].append(copy)

    for turn in range(1, frames + 1):
        peer = lax.rem(frame + turn, frames)
        for head in range(heads):
            cols = slice(head * HD, (head + 1) * HD)
            place = (turn - 1) * heads + head
            numerator = jnp.dot(values[cols, :], probs[place], preferred_element_type=F32)
            result = (numerator / sums[place]).astype(BF16)
            for pair in range(2):
                done[pair, peer, cols, :] = result[:, pair * half : (pair + 1) * half]
        if turn < frames:
            give_back(0, 1 - here, turn)
    for turn in range(1, frames):
        give_back(1, here, turn)
    for pair in range(2):
        back[pair, frame] = done[pair, frame]
    loads[6].wait()

    def collect(step, pair):
        for copy in returns[step]:
            copy.wait_recv()
        rows = pl.ds(pl.multiple_of(pair * half, half), half)
        for source in range(frames):
            att[rows, source * width : (source + 1) * width] = (
                back[pair, source].astype(F32).T.astype(BF16)
            )

    def mixed_term(block, turn):
        if turn == 0:
            collect(0, 1 - here)
        if turn == 2:
            collect(1, here)
        return jnp.dot(att[rows_of(block), :], output_w[...], preferred_element_type=F32)

    mixed = reduce_rows(
        mixed_term, sent.at[1], got_near.at[1], got_far.at[1], sum_send.at[1], sum_recv.at[1]
    )
    out_ref[...] = (hidden.astype(F32) + mixed).astype(BF16)
    for batch in moves + returns:
        for copy in batch:
            copy.wait_send()


def body_fast(
    latents,
    spatial_weight,
    spatial_bias,
    norm_gain,
    norm_shift,
    temporal_weight,
    temporal_bias,
    token_gain,
    query_weight,
    key_weight,
    value_weight,
    output_weight,
):
    channels = latents.shape[3]
    peers, frames = lax.axis_size("rows"), lax.axis_size("frames")
    block = latents.reshape(-1, channels)
    size = block.shape[0]
    tokens = size * peers
    width_cells = latents.shape[2]
    local_out = spatial_weight.shape[3]
    width = query_weight.shape[1] // frames
    heads = width // HD
    links = 2 * PARTS + 1
    denoised = pl.pallas_call(
        functools.partial(block_kernel, frames, width_cells, NORM_GROUPS // peers),
        out_shape=jax.ShapeDtypeStruct(block.shape, BF16),
        in_specs=[ANY_SPEC] * 2
        + [VMEM_SPEC] * 3
        + [ANY_SPEC]
        + [VMEM_SPEC] * 2
        + [ANY_SPEC] * 4,
        out_specs=VMEM_SPEC,
        scratch_shapes=[
            pltpu.VMEM(block.shape, BF16),
            pltpu.VMEM(spatial_weight.shape[:2] + (local_out, channels), BF16),
            pltpu.VMEM(temporal_weight.shape, BF16),
            pltpu.VMEM((3,) + query_weight.shape, BF16),
            pltpu.VMEM(output_weight.shape, BF16),
            pltpu.VMEM((peers,) + block.shape, BF16),
            pltpu.VMEM((3, tokens + 2 * width_cells, channels), BF16),
            pltpu.VMEM((tokens, local_out), F32),
            pltpu.VMEM((tokens, local_out), BF16),
            pltpu.VMEM((2, tokens, local_out), BF16),
            pltpu.VMEM(block.shape, BF16),
            pltpu.VMEM((peers,) + block.shape, BF16),
            pltpu.VMEM((3, 2, frames, width, tokens // 2), BF16),
            pltpu.VMEM((3, 2, frames, width, tokens // 2), BF16),
            pltpu.VMEM((frames * tokens, width), BF16),
            pltpu.VMEM((width, frames * tokens), BF16),
            pltpu.VMEM((frames * heads, frames * tokens, tokens), BF16),
            pltpu.VMEM((2, frames, width, tokens // 2), BF16),
            pltpu.VMEM((2, frames, width, tokens // 2), BF16),
            pltpu.VMEM((tokens, frames * width), BF16),
            pltpu.VMEM((2, 3) + block.shape, BF16),
            pltpu.VMEM((2, 2) + block.shape, BF16),
            pltpu.VMEM((2,) + block.shape, BF16),
            DMA((7,)),
            DMA((links,)),
            DMA((links,)),
            DMA((2, peers)),
            DMA((2, peers)),
            DMA((links,)),
            DMA((links,)),
            DMA((3, 2, frames)),
            DMA((3, 2, frames)),
            DMA((2, frames)),
            DMA((2, frames)),
            DMA((2, 3)),
            DMA((2, 3)),
        ],
        compiler_params=pltpu.CompilerParams(
            collective_id=0, has_side_effects=True, vmem_limit_bytes=VMEM_LIMIT
        ),
    )(
        block,
        jnp.swapaxes(spatial_weight, 2, 3),
        spatial_bias,
        norm_gain,
        norm_shift,
        temporal_weight,
        temporal_bias,
        token_gain,
        query_weight,
        key_weight,
        value_weight,
        output_weight,
    )
    return denoised.reshape(latents.shape)


def fits(mesh):
    def choose(*args):
        latents, query_weight = args[0], args[8]
        peers, frames = mesh.shape["rows"], mesh.shape["frames"]
        heads = query_weight.shape[1] // HD
        tokens = latents.shape[0] * latents.shape[1] * latents.shape[2] * peers
        fast = (
            peers == 4
            and latents.shape[1] == 1
            and heads % frames == 0
            and tokens % 256 == 0
            and latents.shape[2] % 16 == 0
            and latents.shape[0] * latents.shape[2] % (16 * PARTS) == 0
        )
        return (body_fast if fast else body)(*args)

    return choose


def solution(mesh):
    in_specs = (
        P("rows", ("groups", "frames"), None, None),
        P(None, None, None, "rows"),
        P("rows"),
        P("rows"),
        P("rows"),
        P(None, "rows", None),
        P(),
        P(),
        P(None, "rows"),
        P(None, "rows"),
        P(None, "rows"),
        P("rows", None),
    )
    out_specs = P("rows", ("groups", "frames"), None, None)
    return jax.shard_map(
        fits(mesh), mesh=mesh, in_specs=in_specs, out_specs=out_specs, check_vma=False
    )
```
